32 devices in a mesh: depth: 8 (over y, x, core), group: 4 (over z).
Axes of the slice: x: 2, y: 2, z: 4, core: 2. Of those that a mesh axis runs over, the one named last changes fastest.
Arguments:
- output_one: bfloat16 [32, 128, 64, 128], P(None, 'depth', 'group'), may hold values from -6 to 6
- output_two: bfloat16 [32, 128, 64, 128], P(None, 'depth', 'group'), may hold values from -6 to 6
- cotangent_one: bfloat16 [32, 128, 64, 128], P(None, 'depth', 'group'), may hold values from -6 to 6
- cotangent_two: bfloat16 [32, 128, 64, 128], P(None, 'depth', 'group'), may hold values from -6 to 6
- first_weight: bfloat16 [27, 32, 32], replicated, may hold values from -0.21875 to 0.21875
- second_weight: bfloat16 [27, 32, 32], replicated, may hold values from -0.21875 to 0.21875
- bricks: int32 [8, 4, 8], P('depth'), may hold values from 0 to 8, as said below
Outputs:
- restored_one: bfloat16 [32, 128, 64, 128], P(None, 'depth', 'group')
- restored_two: bfloat16 [32, 128, 64, 128], P(None, 'depth', 'group')
- input_grad_one: bfloat16 [32, 128, 64, 128], P(None, 'depth', 'group')
- input_grad_two: bfloat16 [32, 128, 64, 128], P(None, 'depth', 'group')
- first_weight_grad: float32 [27, 32, 32], replicated
- second_weight_grad: float32 [27, 32, 32], replicated
The draws below stay inside these ranges and needn't reach their ends.
Inputs may be any that keep to these rules, and one draw needn't show every extreme that they name: bricks[z, g, :] lists the positions of the occupied bricks of depth layer z and lateral row g, distinct and ascending, followed by 8 in every unused entry. For each z the numbers of occupied bricks over g = 0 .. 3 are a reordering of 1 + (7 * j * j) // 9 for j = 0 .. 3, so in every depth layer one row has all 8 bricks occupied and the layer holds at most 16 occupied bricks.
All inputs are finite; a program needn't handle non-finite values.
Results may differ from the reference program's by a relative error of at most 0.0085.
Values may be sent and summed in bfloat16 or wider, within the bound.
No kernel may reach another device: no remote copies, remote signals or barrier semaphores. Data moves between devices by JAX's collectives and lax.ppermute only.
A program may use at most 256 MiB of HBM per device.

```python
import math
import jax
import jax.numpy as jnp
from jax import lax

CH = 32
B = 16
BX = 8
NBZ = 8
NBY = 4
NZ = 128
NY = 64
NX = 128


def draw_bricks(key, part):
    count_key = jax.random.fold_in(key, 101)
    order_key = jax.random.fold_in(key, 202)
    indices = jnp.arange(NBY, dtype=jnp.int32)
    pattern = 1 + (BX - 1) * indices * indices // ((NBY - 1) * (NBY - 1))
    row_keys = jax.random.split(count_key, NBZ)
    counts = jax.vmap(lambda row_key: jax.random.permutation(row_key, pattern))(row_keys)
    scores = jax.random.randint(order_key, (NBZ, NBY, BX), 0, 1 << 20) * BX + jnp.arange(BX, dtype=jnp.int32)
    shuffled = jnp.argsort(scores, axis=-1).astype(jnp.int32)
    chosen = jnp.where(jnp.arange(BX, dtype=jnp.int32)[None, None, :] < counts[:, :, None], shuffled, BX)
    return jnp.sort(chosen, axis=-1).astype(jnp.int32)


def block_levels(stream_key, shape, cuts, least, high):
    factor_of = 1.0
    for axis_at, blocks in cuts:
        steps = jax.random.uniform(jax.random.fold_in(jax.random.fold_in(stream_key, 6), axis_at), (blocks,), jnp.float32, least / len(cuts), high / len(cuts))
        factor_of = factor_of * jnp.repeat(jnp.exp(steps), shape[axis_at] // blocks).reshape((-1,) + (1,) * (len(shape) - 1 - axis_at))
    return factor_of


def noise(own_key, shape, scale, bound, cuts=(), kind=jnp.bfloat16):
    entries = jax.random.normal(own_key, shape, jnp.float32) * scale
    if len(cuts) > 0:
        entries = block_levels(own_key, shape, cuts, -0.22, 0.18) * entries
    return jnp.clip(entries, min=-bound, max=bound).astype(kind)


def setup_inputs(seed: int = 0) -> dict:
    arg_keys = jax.random.split(jax.random.key(seed), 8)
    return {
        "output_one": noise(arg_keys[0], (CH, NZ, NY, NX), 1.0, 6.0, ((1, 8), (2, 4))),
        "output_two": noise(arg_keys[1], (CH, NZ, NY, NX), 1.0, 6.0, ((1, 8), (2, 4))),
        "cotangent_one": noise(arg_keys[2], (CH, NZ, NY, NX), 1.0, 6.0, ((1, 8), (2, 4))),
        "cotangent_two": noise(arg_keys[3], (CH, NZ, NY, NX), 1.0, 6.0, ((1, 8), (2, 4))),
        "first_weight": noise(arg_keys[4], (27, CH, CH), (27 * CH) ** -0.5, 0.21875),
        "second_weight": noise(arg_keys[5], (27, CH, CH), (27 * CH) ** -0.5, 0.21875),
        "bricks": draw_bricks(jax.random.fold_in(arg_keys[7], 71), 0),
    }


def logistic_slope(inputs):
    logistic = jax.nn.sigmoid(inputs)
    return logistic * (1.0 + inputs * (1.0 - logistic))

def correlate(window, kernel):
    channels_out = kernel.shape[1]
    channels_in = kernel.shape[2]
    shaped_kernel = jnp.transpose(kernel.reshape(3, 3, 3, channels_out, channels_in), (3, 4, 0, 1, 2))
    result = lax.conv_general_dilated(window[None], shaped_kernel, (1, 1, 1), 'VALID', dimension_numbers=('NCDHW', 'OIDHW', 'NCDHW'), precision=lax.Precision.HIGHEST)
    return result[0]

def flipped(kernel):
    return jnp.transpose(jnp.flip(kernel, 0), (0, 2, 1))

def tap_slices(window, brick_edge):
    pieces = []
    for depth_step in range(3):
        for row_step in range(3):
            for col_step in range(3):
                pieces.append(window[:, depth_step:depth_step + brick_edge, row_step:row_step + brick_edge, col_step:col_step + brick_edge])
    return jnp.stack(pieces, axis=0)

def weight_gradient(errors, window, brick_edge):
    return jnp.einsum('ozyx,tizyx->toi', errors, tap_slices(window, brick_edge), precision=lax.Precision.HIGHEST)

def reference(output_one, output_two, cotangent_one, cotangent_two, first_weight, second_weight, bricks):
    window_edge = B + 2
    slots_total = NBZ * NBY * BX
    present = jnp.any(bricks[:, :, :, None] == jnp.arange(BX, dtype=jnp.int32)[None, None, None, :], axis=2)
    present = present.astype(jnp.float32)
    voxel_mask = jnp.repeat(jnp.repeat(jnp.repeat(present, B, axis=0), B, axis=1), B, axis=2)
    first_kernel = first_weight.astype(jnp.float32)
    second_kernel = second_weight.astype(jnp.float32)

    def padded_volume(volume):
        return jnp.pad(volume, ((0, 0), (1, 1), (1, 1), (1, 1)))

    def locate(number):
        depth_index = (number // (NBY * BX)).astype(jnp.int32)
        row_index = (number // BX % NBY).astype(jnp.int32)
        col_index = (number % BX).astype(jnp.int32)
        return (depth_index, row_index, col_index)

    def cut(volume, corner, extent):
        start = (jnp.zeros((), jnp.int32),) + corner
        return lax.dynamic_slice(volume, start, (volume.shape[0], extent, extent, extent)).astype(jnp.float32)

    def place(volume, brick, corner):
        start = (jnp.zeros((), jnp.int32),) + corner
        return lax.dynamic_update_slice(volume, brick.astype(volume.dtype), start)

    def sweep(work, carry):

        def visit(number, state):
            depth_index, row_index, col_index = locate(number)
            corner = ((depth_index * B).astype(jnp.int32), (row_index * B).astype(jnp.int32), (col_index * B).astype(jnp.int32))
            return lax.cond(present[depth_index, row_index, col_index] > 0, lambda inner: work(inner, corner), lambda inner: inner, state)
        return lax.fori_loop(0, slots_total, visit, carry)
    zero_volume = jnp.zeros(output_one.shape, jnp.bfloat16)
    zero_grad = jnp.zeros(second_weight.shape, jnp.float32)
    upper_masked = (output_one.astype(jnp.float32) * voxel_mask).astype(jnp.bfloat16)
    padded_upper = padded_volume(upper_masked)

    def first_work(state, corner):
        shaped, errors, partials = state
        window = cut(padded_upper, corner, window_edge)
        preact = correlate(window, second_kernel)
        cotangent_brick = cut(cotangent_two, corner, B)
        shaped_brick = jax.nn.silu(preact).astype(jnp.bfloat16)
        error_brick = (cotangent_brick * logistic_slope(preact)).astype(jnp.bfloat16)
        partials = partials + weight_gradient(error_brick.astype(jnp.float32), window, B)
        return (place(shaped, shaped_brick, corner), place(errors, error_brick, corner), partials)
    shaped_g, errors_g, second_grad = sweep(first_work, (zero_volume, zero_volume, zero_grad))
    restored_two = (output_two.astype(jnp.float32) - shaped_g.astype(jnp.float32)).astype(jnp.bfloat16)
    lower_masked = (restored_two.astype(jnp.float32) * voxel_mask).astype(jnp.bfloat16)
    padded_lower = padded_volume(lower_masked)
    padded_errors = padded_volume(errors_g)
    second_back = flipped(second_kernel)

    def second_work(state, corner):
        totals, shaped, errors, partials = state
        window = cut(padded_lower, corner, window_edge)
        preact = correlate(window, first_kernel)
        spread = correlate(cut(padded_errors, corner, window_edge), second_back)
        total_brick = (cut(cotangent_one, corner, B) + spread).astype(jnp.bfloat16)
        shaped_brick = jax.nn.silu(preact).astype(jnp.bfloat16)
        error_brick = (total_brick.astype(jnp.float32) * logistic_slope(preact)).astype(jnp.bfloat16)
        partials = partials + weight_gradient(error_brick.astype(jnp.float32), window, B)
        return (place(totals, total_brick, corner), place(shaped, shaped_brick, corner), place(errors, error_brick, corner), partials)
    input_grad_one, shaped_f, errors_f, first_grad = sweep(second_work, (cotangent_one, zero_volume, zero_volume, zero_grad))
    restored_one = (output_one.astype(jnp.float32) - shaped_f.astype(jnp.float32)).astype(jnp.bfloat16)
    padded_last = padded_volume(errors_f)
    first_back = flipped(first_kernel)

    def third_work(state, corner):
        spread = correlate(cut(padded_last, corner, window_edge), first_back)
        return place(state, (cut(cotangent_two, corner, B) + spread).astype(jnp.bfloat16), corner)
    input_grad_two = sweep(third_work, cotangent_two)
    scale = 1.0 / math.sqrt(float(NZ * NY * NX))
    return (restored_one, restored_two, input_grad_one, input_grad_two, first_grad * scale, second_grad * scale)
```

```python
import functools
import math

import jax
import jax.numpy as jnp
from jax import lax
from jax.experimental import pallas as pl
from jax.experimental.pallas import tpu as pltpu
from jax.sharding import PartitionSpec as P

BF = jnp.bfloat16
F32 = jnp.float32
HALF = 8


def shifted(plane, step):
    if step == 0:
        return plane
    width = plane.shape[1]
    lane = lax.broadcasted_iota(jnp.int32, plane.shape, 1)
    edge = 0 if step < 0 else width - 1
    rolled = pltpu.roll(plane, (-step) % width, axis=1)
    return jnp.where(lane == edge, jnp.zeros_like(rolled), rolled)


def picker(rows):
    channels = rows // HALF
    out = lax.broadcasted_iota(jnp.int32, (2 * channels, rows), 0)
    col = lax.broadcasted_iota(jnp.int32, (2 * channels, rows), 1)
    wanted = (out % channels) * HALF + jnp.where(out < channels, 0, HALF - 1)
    return jnp.where(col == wanted, 1.0, 0.0).astype(BF)


def build_field(field, f, centre, halos, width, wanted=(0, 1)):
    zlo, zhi, ylo, yhi = halos
    rows = centre.shape[2]
    channels = rows // HALF
    depth = centre.shape[3] // width
    pick = picker(rows)

    def plane(number, first, second, low, high):
        lanes = pl.ds(pl.multiple_of(number * width, width), width)
        for place, half in enumerate(wanted):
            main, other = (first, second) if half == 0 else (second, first)
            ends = jnp.dot(pick, other, preferred_element_type=F32).astype(BF)
            sides = [low, ends[:channels]] if half == 0 else [ends[channels:], high]
            sides = jnp.concatenate(sides, axis=0)
            for at, step in enumerate((-1, 0, 1)):
                field[place, at * rows : (at + 1) * rows, lanes] = shifted(main, step)
                start = 3 * rows + at * 2 * channels
                field[place, start : start + 2 * channels, lanes] = shifted(sides, step)

    for number, face in ((0, zlo), (depth + 1, zhi)):
        plane(
            number,
            face[f, 0:rows, :],
            face[f, rows : 2 * rows, :],
            face[f, 2 * rows : 2 * rows + channels, :],
            face[f, 2 * rows + channels :, :],
        )

    def inner(number, carry):
        lanes = pl.ds(pl.multiple_of(number * width, width), width)
        plane(number + 1, centre[f, 0, :, lanes], centre[f, 1, :, lanes], ylo[f, :, lanes], yhi[f, :, lanes])
        return carry

    lax.fori_loop(0, depth, inner, 0)


def convolve(field, half, taps, pair, width):
    total = None
    for step in range(3):
        lanes = pl.ds(pl.multiple_of((2 * pair + step) * width, width), 2 * width)
        term = jnp.dot(taps[step], field[half, :, lanes], preferred_element_type=F32)
        total = term if total is None else total + term
    return total


def to_native(first, second, part, width):
    lanes = slice(part * width, (part + 1) * width)
    channels = first.shape[0] // HALF
    return jnp.concatenate(
        [first[:, lanes].reshape(channels, HALF, width), second[:, lanes].reshape(channels, HALF, width)], axis=1
    )


def write_parts(f, pair, planes, outs, depth):
    centre, zlo, zhi, ylo, yhi = outs
    channels, tall, width = planes[0].shape
    rows = channels * HALF
    lanes = pl.ds(pl.multiple_of(pair * 2 * width, width), 2 * width)
    pick = picker(rows)
    halves = []
    for half in range(2):
        block = jnp.concatenate(
            [p[:, half * HALF : (half + 1) * HALF, :].reshape(rows, width) for p in planes], axis=1
        ).astype(BF)
        centre[f, half, :, lanes] = block
        halves.append(block)
    low = jnp.dot(pick, halves[0], preferred_element_type=F32).astype(BF)[:channels]
    high = jnp.dot(pick, halves[1], preferred_element_type=F32).astype(BF)[channels:]
    ylo[f, :, lanes] = low
    yhi[f, :, lanes] = high

    @pl.when(pair == 0)
    def _():
        for half in range(2):
            zlo[f, half * rows : (half + 1) * rows, :] = halves[half][:, :width]

    @pl.when(pair == depth // 2 - 1)
    def _():
        for half in range(2):
            zhi[f, half * rows : (half + 1) * rows, :] = halves[half][:, width:]


def part_shapes(fields, channels, depth, width):
    rows = channels * HALF
    face = (fields, 2 * rows, width)
    side = (fields, channels, depth * width)
    return [(fields, 2, rows, depth * width), face, face, side, side]


def whole_spec(shape):
    return pl.BlockSpec(shape, lambda i: (0,) * len(shape))


def pair_spec(shape):
    channels, _, tall, width = shape
    return pl.BlockSpec((channels, 2, tall, width), lambda i: (0, i, 0, 0))


def params():
    return pltpu.CompilerParams(dimension_semantics=("arbitrary",), vmem_limit_bytes=60 * 1024 * 1024)


def cost(flops, nbytes):
    return pl.CostEstimate(flops=int(flops), bytes_accessed=int(nbytes), transcendentals=0)


def upper_kernel(depth, source, mask, *outs):
    pair = pl.program_id(0)
    m = mask[...][None]
    planes = [source[:, part].astype(F32) * m for part in range(2)]
    write_parts(0, pair, planes, outs, depth)


def upper_parts(source, mask):
    channels, depth, tall, width = source.shape
    shapes = part_shapes(1, channels, depth, width)
    return pl.pallas_call(
        functools.partial(upper_kernel, depth),
        out_shape=[jax.ShapeDtypeStruct(s, BF) for s in shapes],
        grid=(depth // 2,),
        in_specs=[pair_spec(source.shape), whole_spec(mask.shape)],
        out_specs=[whole_spec(s) for s in shapes],
        compiler_params=params(),
        cost_estimate=cost(1e8, 6e6),
        name="upper_parts",
    )(source, mask)


def taps_kernel(taps, out):
    channels = taps.shape[3]
    rows = channels * HALF
    chan = lax.broadcasted_iota(jnp.int32, (channels, rows), 0)
    col = lax.broadcasted_iota(jnp.int32, (channels, rows), 1)
    spread = jnp.where(col // HALF == chan, 1.0, 0.0).astype(BF)
    row_at = lax.broadcasted_iota(jnp.int32, (channels, HALF, rows), 1)
    col_at = lax.broadcasted_iota(jnp.int32, (channels, HALF, rows), 2) % HALF
    gap = col_at - row_at
    width = 6 * channels
    place_row = lax.broadcasted_iota(jnp.int32, (channels, width), 0)
    place_col = lax.broadcasted_iota(jnp.int32, (channels, width), 1)
    side_row = lax.broadcasted_iota(jnp.int32, (channels, HALF, width), 1)
    side_lane = lax.broadcasted_iota(jnp.int32, (channels, HALF, width), 2) // channels % 2
    keep = ((side_row == 0) & (side_lane == 0)) | ((side_row == HALF - 1) & (side_lane == 1))
    for a in range(3):
        for c in range(3):
            wide = [
                jnp.dot(taps[0, 9 * a + 3 * b + c], spread, preferred_element_type=F32)[:, None, :] for b in range(3)
            ]
            block = jnp.where(gap == 0, wide[1], 0.0)
            block = jnp.where(gap == -1, wide[0], block)
            block = jnp.where(gap == 1, wide[2], block)
            out[0, a, :, c * rows : (c + 1) * rows] = block.reshape(rows, rows).astype(BF)
        edge = None
        for c in range(3):
            for end in range(2):
                place = jnp.where(place_col == (2 * c + end) * channels + place_row, 1.0, 0.0).astype(BF)
                term = jnp.dot(taps[0, 9 * a + 6 * end + c], place, preferred_element_type=F32)
                edge = term if edge is None else edge + term
        edge = jnp.where(keep, edge[:, None, :], 0.0)
        out[0, a, :, 3 * rows :] = edge.reshape(rows, width).astype(BF)


def banded(kernels):
    count, taps, channels, _ = kernels.shape
    rows = channels * HALF
    length = 3 * rows + 6 * channels
    return pl.pallas_call(
        taps_kernel,
        out_shape=jax.ShapeDtypeStruct((count, 3, rows, length), BF),
        grid=(count,),
        in_specs=[
            pl.BlockSpec((1, taps, channels, channels), lambda i: (i, 0, 0, 0)),
        ],
        out_specs=pl.BlockSpec((1, 3, rows, length), lambda i: (i, 0, 0, 0)),
        compiler_params=params(),
        cost_estimate=cost(1e9, 8e6),
        name="banded_taps",
    )(kernels)


def first_kernel(depth, width, mask, taps, centre, *refs):
    halos, (output_two, cotangent_two), restored, parts, field = refs[:4], refs[4:6], refs[6], refs[7:12], refs[12]
    pair = pl.program_id(0)

    @pl.when(pair == 0)
    def _():
        build_field(field, 0, centre, halos, width)

    m = mask[...][None]
    sums = [convolve(field, half, taps.at[0], pair, width) for half in range(2)]
    lower, errors = [], []
    for part in range(2):
        preact = to_native(sums[0], sums[1], part, width)
        s = jax.nn.sigmoid(preact)
        shaped = (m * (preact * s)).astype(BF).astype(F32)
        slope = s * (1.0 + preact * (1.0 - s))
        out = (output_two[:, part].astype(F32) - shaped).astype(BF)
        restored[:, part] = out
        lower.append(out.astype(F32) * m)
        errors.append(m * (cotangent_two[:, part].astype(F32) * slope))
    write_parts(0, pair, lower, parts, depth)
    write_parts(1, pair, errors, parts, depth)


def second_kernel(depth, width, mask, taps_f, taps_g, centre, *refs):
    halos, (output_one, cotangent_one) = refs[:4], refs[4:6]
    restored, grad, parts = refs[6], refs[7], refs[8:13]
    field_l, field_e = refs[13], refs[14]
    pair = pl.program_id(0)

    @pl.when(pair == 0)
    def _():
        build_field(field_l, 0, centre, halos, width)
        build_field(field_e, 1, centre, halos, width)

    m = mask[...][None]
    sums = [convolve(field_l, half, taps_f.at[0], pair, width) for half in range(2)]
    spreads = [convolve(field_e, half, taps_g.at[0], pair, width) for half in range(2)]
    errors = []
    for part in range(2):
        preact = to_native(sums[0], sums[1], part, width)
        spread = to_native(spreads[0], spreads[1], part, width)
        s = jax.nn.sigmoid(preact)
        shaped = (m * (preact * s)).astype(BF).astype(F32)
        slope = s * (1.0 + preact * (1.0 - s))
        restored[:, part] = (output_one[:, part].astype(F32) - shaped).astype(BF)
        total = (cotangent_one[:, part].astype(F32) + m * spread).astype(BF)
        grad[:, part] = total
        errors.append(m * (total.astype(F32) * slope))
    write_parts(0, pair, errors, parts, depth)


def third_kernel(depth, width, mask, taps, centre, *refs):
    halos, cotangent_two, grad, field = refs[:4], refs[4], refs[5], refs[6]
    pair = pl.program_id(0)

    @pl.when(pair == 0)
    def _():
        build_field(field, 0, centre, halos, width)

    m = mask[...][None]
    sums = [convolve(field, half, taps.at[0], pair, width) for half in range(2)]
    for part in range(2):
        spread = to_native(sums[0], sums[1], part, width)
        grad[:, part] = (cotangent_two[:, part].astype(F32) + m * spread).astype(BF)


def conv_call(kernel, mask, matrices, centre, halos, natives, n_native_out, out_fields, fields, name):
    channels, depth, tall, width = natives[0].shape
    rows = channels * HALF
    length = matrices[0][0].shape[3]
    shapes = part_shapes(out_fields, channels, depth, width) if out_fields else []
    tap_specs = [
        pl.BlockSpec((1, 3, rows, length), functools.partial(lambda k, i: (k, 0, 0, 0), k)) for _, k in matrices
    ]
    native = natives[0].shape
    return pl.pallas_call(
        functools.partial(kernel, depth, width),
        out_shape=[jax.ShapeDtypeStruct(native, BF)] * n_native_out + [jax.ShapeDtypeStruct(s, BF) for s in shapes],
        grid=(depth // 2,),
        in_specs=[whole_spec(mask.shape)]
        + tap_specs
        + [whole_spec(centre.shape)]
        + [whole_spec(h.shape) for h in halos]
        + [pair_spec(native)] * len(natives),
        out_specs=[pair_spec(native)] * n_native_out + [whole_spec(s) for s in shapes],
        scratch_shapes=[pltpu.VMEM((2, length, (depth + 2) * width), BF)] * fields,
        compiler_params=params(),
        cost_estimate=cost(2 * 2 * rows * 3 * length * depth * width * fields, 2e7),
        name=name,
    )(mask, *[m for m, _ in matrices], centre, *halos, *natives)


def gradient_kernel(depth, width, f, half, centre, *refs):
    halos, errors, out, field = refs[:4], refs[4], refs[5], refs[6]
    rows = centre.shape[2]
    channels = rows // HALF
    a = pl.program_id(0)

    @pl.when(a == 0)
    def _():
        build_field(field, 0, centre, halos, width, (half,))

    lanes = pl.ds(pl.multiple_of(a * width, width), depth * width)

    def product(start, size):
        return lax.dot_general(
            errors[0, half],
            field[0, start : start + size, lanes],
            (((1,), (1,)), ((), ())),
            preferred_element_type=F32,
        ).reshape(channels, HALF, size)

    gap = lax.broadcasted_iota(jnp.int32, (HALF, rows), 1) % HALF - lax.broadcasted_iota(jnp.int32, (HALF, rows), 0)
    picked = {}
    for c in range(3):
        block = product(c * rows, rows)
        for b in range(3):
            picked[b, c] = jnp.sum(jnp.where((gap == b - 1)[None], block, 0.0), axis=1)
    block = product(3 * rows, 6 * channels)
    side_lane = lax.broadcasted_iota(jnp.int32, (channels, 6 * channels), 1) // channels % 2
    sides = jnp.where(side_lane == 0, block[:, 0, :], block[:, HALF - 1, :])
    fold_row = lax.broadcasted_iota(jnp.int32, (rows, channels), 0)
    fold_col = lax.broadcasted_iota(jnp.int32, (rows, channels), 1)
    fold = jnp.where(fold_row // HALF == fold_col, 1.0, 0.0).astype(BF)
    left = jnp.concatenate([picked[b, c] for b in range(3) for c in range(3)], axis=0)
    summed = None
    for _ in range(3):
        piece = left.astype(BF)
        left = left - piece.astype(F32)
        term = jnp.dot(piece, fold, preferred_element_type=F32)
        summed = term if summed is None else summed + term
    values = []
    for b in range(3):
        for c in range(3):
            at = (3 * b + c) * channels
            value = summed[at : at + channels]
            if b != 1:
                at = (2 * c + b // 2) * channels
                value = value + sides[:, at : at + channels]
            values.append(value)
    out[:, pl.ds(pl.multiple_of(a * 8 * channels, 8 * channels), 8 * channels)] = jnp.concatenate(values[:8], axis=1)
    empty = jnp.zeros((channels, channels), F32)
    tail = jnp.concatenate([jnp.where(a == k, values[8], empty) for k in range(3)] + [empty] * 5, axis=1)
    last = slice(24 * channels, 32 * channels)

    @pl.when(a == 0)
    def _():
        out[:, last] = tail

    @pl.when(a > 0)
    def _():
        out[:, last] = out[:, last] + tail


def weight_gradient(centre, halos, f, errors, half, width):
    fields, _, rows, columns = centre.shape
    channels = rows // HALF
    depth = columns // width
    length = 3 * rows + 6 * channels

    def one(shape, which):
        return pl.BlockSpec((1,) + shape[1:], lambda i: (which,) + (0,) * (len(shape) - 1))

    errors, which = errors
    return pl.pallas_call(
        functools.partial(gradient_kernel, depth, width, f, half),
        out_shape=jax.ShapeDtypeStruct((channels, 32 * channels), F32),
        grid=(3,),
        in_specs=[one(centre.shape, f)] + [one(h.shape, f) for h in halos] + [one(errors.shape, which)],
        out_specs=whole_spec((channels, 32 * channels)),
        scratch_shapes=[pltpu.VMEM((1, length, (depth + 2) * width), BF)],
        compiler_params=params(),
        cost_estimate=cost(2 * rows * 3 * length * depth * width, 5e6),
        name="weight_gradient",
    )(centre, *halos, errors)


def unpack_kernel(packed, *outs):
    channels = packed.shape[0]
    for k, out in enumerate(outs):
        for a in range(3):
            for t in range(9):
                at = 8 * a + t if t < 8 else 24 + a
                at = (32 * k + at) * channels
                out[9 * a + t] = packed[:, at : at + channels]


def unpack(packed):
    channels = packed.shape[0]
    shape = (27, channels, channels)
    return pl.pallas_call(
        unpack_kernel,
        out_shape=[jax.ShapeDtypeStruct(shape, F32)] * 2,
        grid=(1,),
        in_specs=[whole_spec(packed.shape)],
        out_specs=[whole_spec(shape)] * 2,
        compiler_params=params(),
        name="unpack",
    )(packed)


def total_over_devices(value, scale):
    axes = ("depth", "group")
    devices = lax.axis_size("depth") * lax.axis_size("group")
    shares = lax.all_to_all(value.reshape(devices, -1, 128), axes, 0, 0)
    share = jnp.sum(shares, axis=0) * scale
    everyone = lax.all_to_all(jnp.broadcast_to(share[None], shares.shape), axes, 0, 0)
    return everyone.reshape(value.shape)


def shift_along(value, axis, step):
    size = lax.axis_size(axis)
    return lax.ppermute(value, axis, [(i + step, i) for i in range(size) if 0 <= i + step < size])


def exchange_sides(faces):
    zlo, zhi, ylo, yhi = faces
    return shift_along(yhi, "group", -1), shift_along(ylo, "group", 1)


def exchange_faces(faces, sides, width):
    zlo, zhi, _, _ = faces
    low, high = sides
    first = jnp.concatenate([zlo, low[:, :, :width], high[:, :, :width]], axis=1)
    last = jnp.concatenate([zhi, low[:, :, -width:], high[:, :, -width:]], axis=1)
    return [shift_along(last, "depth", -1), shift_along(first, "depth", 1), low, high]


def after(value, others):
    return lax.optimization_barrier((value, others))[0]


def local(
    output_one, output_two, cotangent_one, cotangent_two, first_weight, second_weight, bricks
):
    brick_edge = output_one.shape[1]
    width = output_one.shape[3]
    slots = bricks.shape[2]
    groups = lax.axis_size("group")
    position = lax.axis_index("group")
    own_list = bricks[0][position]
    present = jnp.any(own_list[:, None] == jnp.arange(slots, dtype=jnp.int32)[None, :], axis=0)
    mask = jnp.repeat(present.astype(F32), brick_edge)[None, :]

    upper, *faces = upper_parts(output_one, mask)
    sides = exchange_sides(faces)

    def turned(kernel):
        return jnp.transpose(jnp.flip(kernel, 0), (0, 2, 1))

    taps_g = banded(jnp.stack([second_weight, turned(second_weight)]))
    sides = after(sides, taps_g)
    upper_halos = exchange_faces(faces, sides, width)
    taps_f = banded(jnp.stack([first_weight, turned(first_weight)]))

    restored_two, middle, *faces = conv_call(
        first_kernel, mask, [(taps_g, 0)], upper, upper_halos, [output_two, cotangent_two], 1, 2, 1, "first_conv"
    )
    sides = exchange_sides(faces)
    second_a = weight_gradient(upper, upper_halos, 0, (middle, 1), 0, width)
    sides = after(sides, second_a)
    middle_halos = exchange_faces(faces, sides, width)
    second_b = weight_gradient(upper, upper_halos, 0, (middle, 1), 1, width)
    restored_one, input_grad_one, last, *faces = conv_call(
        second_kernel,
        mask,
        [(taps_f, 0), (taps_g, 1)],
        middle,
        middle_halos,
        [output_one, cotangent_one],
        2,
        1,
        2,
        "second_conv",
    )
    sides = exchange_sides(faces)
    first_a = weight_gradient(middle, middle_halos, 0, (last, 0), 0, width)
    sides = after(sides, first_a)
    last_halos = exchange_faces(faces, sides, width)
    first_b = weight_gradient(middle, middle_halos, 0, (last, 0), 1, width)
    (input_grad_two,) = conv_call(
        third_kernel, mask, [(taps_f, 1)], last, last_halos, [cotangent_two], 1, 0, 1, "third_conv"
    )
    scale = 1.0 / math.sqrt(
        float(brick_edge * lax.axis_size("depth") * output_one.shape[2] * groups * width)
    )
    packed = jnp.concatenate([first_a + first_b, second_a + second_b], axis=1)
    first_total, second_total = unpack(total_over_devices(packed, scale))
    return (restored_one, restored_two, input_grad_one, input_grad_two, first_total, second_total)


def solution(mesh):
    slab = P(None, "depth", "group", None)
    return jax.shard_map(
        local,
        mesh=mesh,
        in_specs=(slab, slab, slab, slab, P(), P(), P("depth", None, None)),
        out_specs=(slab, slab, slab, slab, P(), P()),
        check_vma=False,
    )
```

```python
import functools
import math

import jax
import jax.numpy as jnp
from jax import lax
from jax.experimental import pallas as pl
from jax.experimental.pallas import tpu as pltpu
from jax.sharding import PartitionSpec as P

BF = jnp.bfloat16
F32 = jnp.float32
HALF = 8


def shifted(plane, step):
    if step == 0:
        return plane
    width = plane.shape[1]
    lane = lax.broadcasted_iota(jnp.int32, plane.shape, 1)
    edge = 0 if step < 0 else width - 1
    rolled = pltpu.roll(plane, (-step) % width, axis=1)
    return jnp.where(lane == edge, jnp.zeros_like(rolled), rolled)


def picker(rows):
    channels = rows // HALF
    out = lax.broadcasted_iota(jnp.int32, (2 * channels, rows), 0)
    col = lax.broadcasted_iota(jnp.int32, (2 * channels, rows), 1)
    wanted = (out % channels) * HALF + jnp.where(out < channels, 0, HALF - 1)
    return jnp.where(col == wanted, 1.0, 0.0).astype(BF)


def build_field(field, f, centre, halos, width):
    zlo, zhi, ylo, yhi = halos
    rows = centre.shape[2]
    channels = rows // HALF
    depth = centre.shape[3] // width
    pick = picker(rows)

    def plane(number, first, second, low, high):
        lanes = pl.ds(pl.multiple_of(number * width, width), width)
        for half in range(2):
            main, other = (first, second) if half == 0 else (second, first)
            ends = jnp.dot(pick, other, preferred_element_type=F32).astype(BF)
            sides = [low, ends[:channels]] if half == 0 else [ends[channels:], high]
            sides = jnp.concatenate(sides, axis=0)
            for at, step in enumerate((-1, 0, 1)):
                field[half, at * rows : (at + 1) * rows, lanes] = shifted(main, step)
                start = 3 * rows + at * 2 * channels
                field[half, start : start + 2 * channels, lanes] = shifted(sides, step)

    for number, face in ((0, zlo), (depth + 1, zhi)):
        plane(
            number,
            face[f, 0:rows, :],
            face[f, rows : 2 * rows, :],
            face[f, 2 * rows : 2 * rows + channels, :],
            face[f, 2 * rows + channels :, :],
        )

    def inner(number, carry):
        lanes = pl.ds(pl.multiple_of(number * width, width), width)
        plane(number + 1, centre[f, 0, :, lanes], centre[f, 1, :, lanes], ylo[f, :, lanes], yhi[f, :, lanes])
        return carry

    lax.fori_loop(0, depth, inner, 0, unroll=2)


def convolve(field, half, taps, pair, width):
    total = None
    for step in range(3):
        lanes = pl.ds(pl.multiple_of((2 * pair + step) * width, width), 2 * width)
        term = jnp.dot(taps[step], field[half, :, lanes], preferred_element_type=F32)
        total = term if total is None else total + term
    return total


def to_native(first, second, part, width):
    lanes = slice(part * width, (part + 1) * width)
    channels = first.shape[0] // HALF
    return jnp.concatenate(
        [first[:, lanes].reshape(channels, HALF, width), second[:, lanes].reshape(channels, HALF, width)], axis=1
    )


def write_parts(f, pair, planes, outs, depth):
    centre, zlo, zhi, ylo, yhi = outs
    channels, tall, width = planes[0].shape
    rows = channels * HALF
    lanes = pl.ds(pl.multiple_of(pair * 2 * width, width), 2 * width)
    pick = picker(rows)
    halves = []
    for half in range(2):
        block = jnp.concatenate(
            [p[:, half * HALF : (half + 1) * HALF, :].reshape(rows, width) for p in planes], axis=1
        ).astype(BF)
        centre[f, half, :, lanes] = block
        halves.append(block)
    low = jnp.dot(pick, halves[0], preferred_element_type=F32).astype(BF)[:channels]
    high = jnp.dot(pick, halves[1], preferred_element_type=F32).astype(BF)[channels:]
    ylo[f, :, lanes] = low
    yhi[f, :, lanes] = high

    @pl.when(pair == 0)
    def _():
        for half in range(2):
            zlo[f, half * rows : (half + 1) * rows, :] = halves[half][:, :width]

    @pl.when(pair == depth // 2 - 1)
    def _():
        for half in range(2):
            zhi[f, half * rows : (half + 1) * rows, :] = halves[half][:, width:]


def part_shapes(fields, channels, depth, width):
    rows = channels * HALF
    face = (fields, 2 * rows, width)
    side = (fields, channels, depth * width)
    return [(fields, 2, rows, depth * width), face, face, side, side]


def whole_spec(shape):
    return pl.BlockSpec(shape, lambda i: (0,) * len(shape))


def pair_spec(shape):
    channels, _, tall, width = shape
    return pl.BlockSpec((channels, 2, tall, width), lambda i: (0, i, 0, 0))


def params():
    return pltpu.CompilerParams(dimension_semantics=("arbitrary",), vmem_limit_bytes=60 * 1024 * 1024)


def cost(flops, nbytes):
    return pl.CostEstimate(flops=int(flops), bytes_accessed=int(nbytes), transcendentals=0)


def upper_kernel(depth, source, mask, *outs):
    pair = pl.program_id(0)
    m = mask[...][None]
    planes = [source[:, part].astype(F32) * m for part in range(2)]
    write_parts(0, pair, planes, outs, depth)


def upper_parts(source, mask):
    channels, depth, tall, width = source.shape
    shapes = part_shapes(1, channels, depth, width)
    return pl.pallas_call(
        functools.partial(upper_kernel, depth),
        out_shape=[jax.ShapeDtypeStruct(s, BF) for s in shapes],
        grid=(depth // 2,),
        in_specs=[pair_spec(source.shape), whole_spec(mask.shape)],
        out_specs=[whole_spec(s) for s in shapes],
        compiler_params=params(),
        cost_estimate=cost(1e8, 6e6),
        name="upper_parts",
    )(source, mask)


def taps_kernel(taps, out):
    channels = taps.shape[3]
    rows = channels * HALF
    chan = lax.broadcasted_iota(jnp.int32, (channels, rows), 0)
    col = lax.broadcasted_iota(jnp.int32, (channels, rows), 1)
    spread = jnp.where(col // HALF == chan, 1.0, 0.0).astype(BF)
    row_at = lax.broadcasted_iota(jnp.int32, (channels, HALF, rows), 1)
    col_at = lax.broadcasted_iota(jnp.int32, (channels, HALF, rows), 2) % HALF
    gap = col_at - row_at
    width = 6 * channels
    place_row = lax.broadcasted_iota(jnp.int32, (channels, width), 0)
    place_col = lax.broadcasted_iota(jnp.int32, (channels, width), 1)
    side_row = lax.broadcasted_iota(jnp.int32, (channels, HALF, width), 1)
    side_lane = lax.broadcasted_iota(jnp.int32, (channels, HALF, width), 2) // channels % 2
    keep = ((side_row == 0) & (side_lane == 0)) | ((side_row == HALF - 1) & (side_lane == 1))
    for a in range(3):
        for c in range(3):
            wide = [
                jnp.dot(taps[0, 9 * a + 3 * b + c], spread, preferred_element_type=F32)[:, None, :] for b in range(3)
            ]
            block = jnp.where(gap == 0, wide[1], 0.0)
            block = jnp.where(gap == -1, wide[0], block)
            block = jnp.where(gap == 1, wide[2], block)
            out[0, a, :, c * rows : (c + 1) * rows] = block.reshape(rows, rows).astype(BF)
        edge = None
        for c in range(3):
            for end in range(2):
                place = jnp.where(place_col == (2 * c + end) * channels + place_row, 1.0, 0.0).astype(BF)
                term = jnp.dot(taps[0, 9 * a + 6 * end + c], place, preferred_element_type=F32)
                edge = term if edge is None else edge + term
        edge = jnp.where(keep, edge[:, None, :], 0.0)
        out[0, a, :, 3 * rows :] = edge.reshape(rows, width).astype(BF)


def banded(kernels):
    count, taps, channels, _ = kernels.shape
    rows = channels * HALF
    length = 3 * rows + 6 * channels
    return pl.pallas_call(
        taps_kernel,
        out_shape=jax.ShapeDtypeStruct((count, 3, rows, length), BF),
        grid=(count,),
        in_specs=[
            pl.BlockSpec((1, taps, channels, channels), lambda i: (i, 0, 0, 0)),
        ],
        out_specs=pl.BlockSpec((1, 3, rows, length), lambda i: (i, 0, 0, 0)),
        compiler_params=params(),
        cost_estimate=cost(1e9, 8e6),
        name="banded_taps",
    )(kernels)


def first_kernel(depth, width, mask, taps, centre, *refs):
    halos, (output_two, cotangent_two), restored, parts, field = refs[:4], refs[4:6], refs[6], refs[7:12], refs[13]
    pair = pl.program_id(0)
    kept = pltpu.make_async_copy(field, refs[12], refs[14])

    @pl.when(pair == 0)
    def _():
        build_field(field, 0, centre, halos, width)
        kept.start()

    m = mask[...][None]
    sums = [convolve(field, half, taps.at[0], pair, width) for half in range(2)]
    lower, errors = [], []
    for part in range(2):
        preact = to_native(sums[0], sums[1], part, width)
        s = jax.nn.sigmoid(preact)
        shaped = (m * (preact * s)).astype(BF).astype(F32)
        slope = s * (1.0 + preact * (1.0 - s))
        out = (output_two[:, part].astype(F32) - shaped).astype(BF)
        restored[:, part] = out
        lower.append(out.astype(F32) * m)
        errors.append(m * (cotangent_two[:, part].astype(F32) * slope))
    write_parts(0, pair, lower, parts, depth)
    write_parts(1, pair, errors, parts, depth)

    @pl.when(pair == depth // 2 - 1)
    def _():
        kept.wait()


def second_kernel(depth, width, mask, taps_f, taps_g, centre, *refs):
    halos, (output_one, cotangent_one) = refs[:4], refs[4:6]
    restored, grad, parts = refs[6], refs[7], refs[8:13]
    field_l, field_e = refs[14], refs[15]
    kept = pltpu.make_async_copy(field_l, refs[13], refs[16])
    pair = pl.program_id(0)

    @pl.when(pair == 0)
    def _():
        build_field(field_l, 0, centre, halos, width)
        kept.start()
        build_field(field_e, 1, centre, halos, width)

    m = mask[...][None]
    sums = [convolve(field_l, half, taps_f.at[0], pair, width) for half in range(2)]
    spreads = [convolve(field_e, half, taps_g.at[0], pair, width) for half in range(2)]
    errors = []
    for part in range(2):
        preact = to_native(sums[0], sums[1], part, width)
        spread = to_native(spreads[0], spreads[1], part, width)
        s = jax.nn.sigmoid(preact)
        shaped = (m * (preact * s)).astype(BF).astype(F32)
        slope = s * (1.0 + preact * (1.0 - s))
        restored[:, part] = (output_one[:, part].astype(F32) - shaped).astype(BF)
        total = (cotangent_one[:, part].astype(F32) + m * spread).astype(BF)
        grad[:, part] = total
        errors.append(m * (total.astype(F32) * slope))
    write_parts(0, pair, errors, parts, depth)

    @pl.when(pair == depth // 2 - 1)
    def _():
        kept.wait()


def third_kernel(depth, width, mask, taps, centre, *refs):
    halos, cotangent_two, grad, field = refs[:4], refs[4], refs[5], refs[6]
    pair = pl.program_id(0)

    @pl.when(pair == 0)
    def _():
        build_field(field, 0, centre, halos, width)

    m = mask[...][None]
    sums = [convolve(field, half, taps.at[0], pair, width) for half in range(2)]
    for part in range(2):
        spread = to_native(sums[0], sums[1], part, width)
        grad[:, part] = (cotangent_two[:, part].astype(F32) + m * spread).astype(BF)


def conv_call(kernel, mask, matrices, centre, halos, natives, n_native_out, out_fields, fields, name):
    channels, depth, tall, width = natives[0].shape
    rows = channels * HALF
    length = matrices[0][0].shape[3]
    shapes = part_shapes(out_fields, channels, depth, width) if out_fields else []
    tap_specs = [
        pl.BlockSpec((1, 3, rows, length), functools.partial(lambda k, i: (k, 0, 0, 0), k)) for _, k in matrices
    ]
    native = natives[0].shape
    held = (2, length, (depth + 2) * width)
    export = 1 if out_fields else 0
    return pl.pallas_call(
        functools.partial(kernel, depth, width),
        out_shape=[jax.ShapeDtypeStruct(native, BF)] * n_native_out + [jax.ShapeDtypeStruct(s, BF) for s in shapes]
        + [jax.ShapeDtypeStruct(held, BF)] * export,
        grid=(depth // 2,),
        in_specs=[whole_spec(mask.shape)]
        + tap_specs
        + [whole_spec(centre.shape)]
        + [whole_spec(h.shape) for h in halos]
        + [pair_spec(native)] * len(natives),
        out_specs=[pair_spec(native)] * n_native_out
        + [whole_spec(s) for s in shapes]
        + [pl.BlockSpec(memory_space=pl.ANY)] * export,
        scratch_shapes=[pltpu.VMEM(held, BF)] * fields + [pltpu.SemaphoreType.DMA] * export,
        compiler_params=params(),
        cost_estimate=cost(2 * 2 * rows * 3 * length * depth * width * fields, 2e7),
        name=name,
    )(mask, *[m for m, _ in matrices], centre, *halos, *natives)


def gradient_kernel(depth, width, field, errors, out, products):
    rows = errors.shape[2]
    channels = rows // HALF
    a = pl.program_id(0)
    lanes = pl.ds(pl.multiple_of(a * width, width), depth * width)

    products[...] = lax.dot_general(
        errors[0, 0], field[0, :, lanes], (((1,), (1,)), ((), ())), preferred_element_type=F32
    )

    def pieces(value):
        high = value.astype(BF)
        return high, (value - high.astype(F32)).astype(BF)

    def tile(size):
        row = lax.broadcasted_iota(jnp.int32, (2 * HALF, size), 0) % HALF
        return row, lax.broadcasted_iota(jnp.int32, (2 * HALF, size), 1)

    gather_row = lax.broadcasted_iota(jnp.int32, (channels, rows), 0)
    gather_col = lax.broadcasted_iota(jnp.int32, (channels, rows), 1)
    gather = jnp.where(gather_col // HALF == gather_row, 1.0, 0.0).astype(BF)

    def chosen(parts, keep):
        total = None
        for part in parts:
            size = part.shape[1]
            kept = (part.reshape(rows // (2 * HALF), 2 * HALF, size) * keep[None]).reshape(rows, size)
            term = jnp.dot(gather, kept, preferred_element_type=F32)
            total = term if total is None else total + term
        return total

    row, col = tile(rows)
    bands = [jnp.where(col % HALF - row == b - 1, 1.0, 0.0).astype(BF) for b in range(3)]
    picked = {}
    for c in range(3):
        parts = pieces(products[:, c * rows : (c + 1) * rows])
        for b in range(3):
            picked[b, c] = chosen(parts, bands[b])
    row, col = tile(6 * channels)
    ends = jnp.where(row == jnp.where(col // channels % 2 == 0, 0, HALF - 1), 1.0, 0.0).astype(BF)
    sides = chosen(pieces(products[:, 3 * rows :]), ends)
    fold_row = lax.broadcasted_iota(jnp.int32, (rows, channels), 0)
    fold_col = lax.broadcasted_iota(jnp.int32, (rows, channels), 1)
    fold = jnp.where(fold_row // HALF == fold_col, 1.0, 0.0).astype(BF)
    summed = None
    for piece in pieces(jnp.concatenate([picked[b, c] for b in range(3) for c in range(3)], axis=0)):
        term = jnp.dot(piece, fold, preferred_element_type=F32)
        summed = term if summed is None else summed + term
    values = []
    for b in range(3):
        for c in range(3):
            at = (3 * b + c) * channels
            value = summed[at : at + channels]
            if b != 1:
                at = (2 * c + b // 2) * channels
                value = value + sides[:, at : at + channels]
            values.append(value)
    out[:, pl.ds(pl.multiple_of(a * 8 * channels, 8 * channels), 8 * channels)] = jnp.concatenate(values[:8], axis=1)
    empty = jnp.zeros((channels, channels), F32)
    tail = jnp.concatenate([jnp.where(a == k, values[8], empty) for k in range(3)] + [empty] * 5, axis=1)
    last = slice(24 * channels, 32 * channels)

    @pl.when(a == 0)
    def _():
        out[:, last] = tail

    @pl.when(a > 0)
    def _():
        out[:, last] = out[:, last] + tail


def weight_gradient(field, errors, which, half, width):
    _, length, columns = field.shape
    rows = errors.shape[2]
    channels = rows // HALF
    depth = errors.shape[3] // width
    return pl.pallas_call(
        functools.partial(gradient_kernel, depth, width),
        out_shape=jax.ShapeDtypeStruct((channels, 32 * channels), F32),
        grid=(3,),
        in_specs=[
            pl.BlockSpec((1, length, columns), lambda i: (half, 0, 0)),
            pl.BlockSpec((1, 1, rows, depth * width), lambda i: (which, half, 0, 0)),
        ],
        out_specs=whole_spec((channels, 32 * channels)),
        scratch_shapes=[pltpu.VMEM((rows, length), F32)],
        compiler_params=params(),
        cost_estimate=cost(2 * rows * 3 * length * depth * width, 5e6),
        name="weight_gradient",
    )(field, errors)


def unpack_kernel(packed, *outs):
    channels = packed.shape[0]
    for k, out in enumerate(outs):
        for a in range(3):
            for t in range(9):
                at = 8 * a + t if t < 8 else 24 + a
                at = (32 * k + at) * channels
                out[9 * a + t] = packed[:, at : at + channels]


def unpack(packed):
    channels = packed.shape[0]
    shape = (27, channels, channels)
    return pl.pallas_call(
        unpack_kernel,
        out_shape=[jax.ShapeDtypeStruct(shape, F32)] * 2,
        grid=(1,),
        in_specs=[whole_spec(packed.shape)],
        out_specs=[whole_spec(shape)] * 2,
        compiler_params=params(),
        name="unpack",
    )(packed)


def total_over_devices(value, scale):
    axes = ("depth", "group")
    devices = lax.axis_size("depth") * lax.axis_size("group")
    shares = lax.all_to_all(value.reshape(devices, -1, 128), axes, 0, 0)
    share = jnp.sum(shares, axis=0) * scale
    everyone = lax.all_to_all(jnp.broadcast_to(share[None], shares.shape), axes, 0, 0)
    return everyone.reshape(value.shape)


def shift_along(value, axis, step):
    size = lax.axis_size(axis)
    return lax.ppermute(value, axis, [(i + step, i) for i in range(size) if 0 <= i + step < size])


def exchange_sides(faces):
    zlo, zhi, ylo, yhi = faces
    return shift_along(yhi, "group", -1), shift_along(ylo, "group", 1)


def exchange_faces(faces, sides, width):
    zlo, zhi, _, _ = faces
    low, high = sides
    first = jnp.concatenate([zlo, low[:, :, :width], high[:, :, :width]], axis=1)
    last = jnp.concatenate([zhi, low[:, :, -width:], high[:, :, -width:]], axis=1)
    return [shift_along(last, "depth", -1), shift_along(first, "depth", 1), low, high]


def after(value, others):
    return lax.optimization_barrier((value, others))[0]


def local(
    output_one, output_two, cotangent_one, cotangent_two, first_weight, second_weight, bricks
):
    brick_edge = output_one.shape[1]
    width = output_one.shape[3]
    slots = bricks.shape[2]
    groups = lax.axis_size("group")
    position = lax.axis_index("group")
    own_list = bricks[0][position]
    present = jnp.any(own_list[:, None] == jnp.arange(slots, dtype=jnp.int32)[None, :], axis=0)
    mask = jnp.repeat(present.astype(F32), brick_edge)[None, :]

    upper, *faces = upper_parts(output_one, mask)
    sides = exchange_sides(faces)

    def turned(kernel):
        return jnp.transpose(jnp.flip(kernel, 0), (0, 2, 1))

    taps_g = banded(jnp.stack([second_weight, turned(second_weight)]))
    sides = after(sides, taps_g)
    upper_halos = exchange_faces(faces, sides, width)
    taps_f = banded(jnp.stack([first_weight, turned(first_weight)]))

    restored_two, middle, *faces, field = conv_call(
        first_kernel, mask, [(taps_g, 0)], upper, upper_halos, [output_two, cotangent_two], 1, 2, 1, "first_conv"
    )
    sides = exchange_sides(faces)
    second_a = weight_gradient(field, middle, 1, 0, width)
    sides = after(sides, second_a)
    middle_halos = exchange_faces(faces, sides, width)
    second_b = weight_gradient(field, middle, 1, 1, width)
    restored_one, input_grad_one, last, *faces, field = conv_call(
        second_kernel,
        mask,
        [(taps_f, 0), (taps_g, 1)],
        middle,
        middle_halos,
        [output_one, cotangent_one],
        2,
        1,
        2,
        "second_conv",
    )
    sides = exchange_sides(faces)
    first_a = weight_gradient(field, last, 0, 0, width)
    sides = after(sides, first_a)
    last_halos = exchange_faces(faces, sides, width)
    first_b = weight_gradient(field, last, 0, 1, width)
    (input_grad_two,) = conv_call(
        third_kernel, mask, [(taps_f, 1)], last, last_halos, [cotangent_two], 1, 0, 1, "third_conv"
    )
    scale = 1.0 / math.sqrt(
        float(brick_edge * lax.axis_size("depth") * output_one.shape[2] * groups * width)
    )
    packed = jnp.concatenate([first_a + first_b, second_a + second_b], axis=1)
    first_total, second_total = unpack(total_over_devices(packed, scale))
    return (restored_one, restored_two, input_grad_one, input_grad_two, first_total, second_total)


def solution(mesh):
    slab = P(None, "depth", "group", None)
    return jax.shard_map(
        local,
        mesh=mesh,
        in_specs=(slab, slab, slab, slab, P(), P(), P("depth", None, None)),
        out_specs=(slab, slab, slab, slab, P(), P()),
        check_vma=False,
    )
```

```python
import functools
import math

import jax
import jax.numpy as jnp
from jax import lax
from jax.experimental import pallas as pl
from jax.experimental.pallas import tpu as pltpu
from jax.sharding import PartitionSpec as P

BF = jnp.bfloat16
F32 = jnp.float32
HALF = 8


def shifted(plane, step):
    if step == 0:
        return plane
    width = plane.shape[1]
    lane = lax.broadcasted_iota(jnp.int32, plane.shape, 1)
    edge = 0 if step < 0 else width - 1
    rolled = pltpu.roll(plane, (-step) % width, axis=1)
    return jnp.where(lane == edge, jnp.zeros_like(rolled), rolled)


def picker(rows):
    channels = rows // HALF
    out = lax.broadcasted_iota(jnp.int32, (2 * channels, rows), 0)
    col = lax.broadcasted_iota(jnp.int32, (2 * channels, rows), 1)
    wanted = (out % channels) * HALF + jnp.where(out < channels, 0, HALF - 1)
    return jnp.where(col == wanted, 1.0, 0.0).astype(BF)


def build_field(field, f, centre, halos, width):
    zlo, zhi, ylo, yhi = halos
    rows = centre.shape[2]
    channels = rows // HALF
    depth = centre.shape[3] // width
    pick = picker(rows)

    def plane(number, first, second, low, high):
        lanes = pl.ds(pl.multiple_of(number * width, width), width)
        for half in range(2):
            main, other = (first, second) if half == 0 else (second, first)
            ends = jnp.dot(pick, other, preferred_element_type=F32).astype(BF)
            sides = [low, ends[:channels]] if half == 0 else [ends[channels:], high]
            sides = jnp.concatenate(sides, axis=0)
            for at, step in enumerate((-1, 0, 1)):
                field[half, at * rows : (at + 1) * rows, lanes] = shifted(main, step)
                start = 3 * rows + at * 2 * channels
                field[half, start : start + 2 * channels, lanes] = shifted(sides, step)

    for number, face in ((0, zlo), (depth + 1, zhi)):
        plane(
            number,
            face[f, 0:rows, :],
            face[f, rows : 2 * rows, :],
            face[f, 2 * rows : 2 * rows + channels, :],
            face[f, 2 * rows + channels :, :],
        )

    def inner(number, carry):
        lanes = pl.ds(pl.multiple_of(number * width, width), width)
        plane(number + 1, centre[f, 0, :, lanes], centre[f, 1, :, lanes], ylo[f, :, lanes], yhi[f, :, lanes])
        return carry

    lax.fori_loop(0, depth, inner, 0, unroll=2)


def convolve(field, half, taps, pair, width):
    total = None
    for step in range(3):
        lanes = pl.ds(pl.multiple_of((2 * pair + step) * width, width), 2 * width)
        term = jnp.dot(taps[step], field[half, :, lanes], preferred_element_type=F32)
        total = term if total is None else total + term
    return total


def to_native(first, second, part, width):
    lanes = slice(part * width, (part + 1) * width)
    channels = first.shape[0] // HALF
    return jnp.concatenate(
        [first[:, lanes].reshape(channels, HALF, width), second[:, lanes].reshape(channels, HALF, width)], axis=1
    )


def write_parts(f, pair, planes, outs, depth):
    centre, zlo, zhi, ylo, yhi = outs
    channels, tall, width = planes[0].shape
    rows = channels * HALF
    lanes = pl.ds(pl.multiple_of(pair * 2 * width, width), 2 * width)
    pick = picker(rows)
    halves = []
    for half in range(2):
        block = jnp.concatenate(
            [p[:, half * HALF : (half + 1) * HALF, :].reshape(rows, width) for p in planes], axis=1
        ).astype(BF)
        centre[f, half] = block
        halves.append(block)
    low = jnp.dot(pick, halves[0], preferred_element_type=F32).astype(BF)[:channels]
    high = jnp.dot(pick, halves[1], preferred_element_type=F32).astype(BF)[channels:]
    ylo[f, :, lanes] = low
    yhi[f, :, lanes] = high

    @pl.when(pair == 0)
    def _():
        for half in range(2):
            zlo[f, half * rows : (half + 1) * rows, :] = halves[half][:, :width]

    @pl.when(pair == depth // 2 - 1)
    def _():
        for half in range(2):
            zhi[f, half * rows : (half + 1) * rows, :] = halves[half][:, width:]


def part_shapes(fields, channels, depth, width):
    rows = channels * HALF
    face = (fields, 2 * rows, width)
    side = (fields, channels, depth * width)
    return [(fields, 2, rows, depth * width), face, face, side, side]


def whole_spec(shape):
    return pl.BlockSpec(shape, lambda i: (0,) * len(shape))


def part_specs(shapes, width):
    fields, halves, rows, _ = shapes[0]
    centre = pl.BlockSpec((fields, halves, rows, 2 * width), lambda i: (0, 0, 0, i))
    return [centre] + [whole_spec(s) for s in shapes[1:]]


def pair_spec(shape):
    channels, _, tall, width = shape
    return pl.BlockSpec((channels, 2, tall, width), lambda i: (0, i, 0, 0))


def params():
    return pltpu.CompilerParams(dimension_semantics=("arbitrary",), vmem_limit_bytes=60 * 1024 * 1024)


def cost(flops, nbytes):
    return pl.CostEstimate(flops=int(flops), bytes_accessed=int(nbytes), transcendentals=0)


def upper_kernel(depth, source, mask, *outs):
    pair = pl.program_id(0)
    m = mask[...][None]
    planes = [source[:, part].astype(F32) * m for part in range(2)]
    write_parts(0, pair, planes, outs, depth)


def upper_parts(source, mask):
    channels, depth, tall, width = source.shape
    shapes = part_shapes(1, channels, depth, width)
    return pl.pallas_call(
        functools.partial(upper_kernel, depth),
        out_shape=[jax.ShapeDtypeStruct(s, BF) for s in shapes],
        grid=(depth // 2,),
        in_specs=[pair_spec(source.shape), whole_spec(mask.shape)],
        out_specs=part_specs(shapes, width),
        compiler_params=params(),
        cost_estimate=cost(1e8, 6e6),
        name="upper_parts",
    )(source, mask)


def taps_kernel(taps, out):
    channels = taps.shape[3]
    rows = channels * HALF
    chan = lax.broadcasted_iota(jnp.int32, (channels, rows), 0)
    col = lax.broadcasted_iota(jnp.int32, (channels, rows), 1)
    spread = jnp.where(col // HALF == chan, 1.0, 0.0).astype(BF)
    row_at = lax.broadcasted_iota(jnp.int32, (channels, HALF, rows), 1)
    col_at = lax.broadcasted_iota(jnp.int32, (channels, HALF, rows), 2) % HALF
    gap = col_at - row_at
    width = 6 * channels
    place_row = lax.broadcasted_iota(jnp.int32, (channels, width), 0)
    place_col = lax.broadcasted_iota(jnp.int32, (channels, width), 1)
    side_row = lax.broadcasted_iota(jnp.int32, (channels, HALF, width), 1)
    side_lane = lax.broadcasted_iota(jnp.int32, (channels, HALF, width), 2) // channels % 2
    keep = ((side_row == 0) & (side_lane == 0)) | ((side_row == HALF - 1) & (side_lane == 1))
    for a in range(3):
        for c in range(3):
            wide = [
                jnp.dot(taps[0, 9 * a + 3 * b + c], spread, preferred_element_type=F32)[:, None, :] for b in range(3)
            ]
            block = jnp.where(gap == 0, wide[1], 0.0)
            block = jnp.where(gap == -1, wide[0], block)
            block = jnp.where(gap == 1, wide[2], block)
            out[0, a, :, c * rows : (c + 1) * rows] = block.reshape(rows, rows).astype(BF)
        edge = None
        for c in range(3):
            for end in range(2):
                place = jnp.where(place_col == (2 * c + end) * channels + place_row, 1.0, 0.0).astype(BF)
                term = jnp.dot(taps[0, 9 * a + 6 * end + c], place, preferred_element_type=F32)
                edge = term if edge is None else edge + term
        edge = jnp.where(keep, edge[:, None, :], 0.0)
        out[0, a, :, 3 * rows :] = edge.reshape(rows, width).astype(BF)


def banded(kernels):
    count, taps, channels, _ = kernels.shape
    rows = channels * HALF
    length = 3 * rows + 6 * channels
    return pl.pallas_call(
        taps_kernel,
        out_shape=jax.ShapeDtypeStruct((count, 3, rows, length), BF),
        grid=(count,),
        in_specs=[
            pl.BlockSpec((1, taps, channels, channels), lambda i: (i, 0, 0, 0)),
        ],
        out_specs=pl.BlockSpec((1, 3, rows, length), lambda i: (i, 0, 0, 0)),
        compiler_params=params(),
        cost_estimate=cost(1e9, 8e6),
        name="banded_taps",
    )(kernels)


def first_kernel(depth, width, mask, taps, centre, *refs):
    halos, (output_two, cotangent_two), restored, parts, field = refs[:4], refs[4:6], refs[6], refs[7:12], refs[13]
    pair = pl.program_id(0)
    kept = pltpu.make_async_copy(field, refs[12], refs[14])

    @pl.when(pair == 0)
    def _():
        build_field(field, 0, centre, halos, width)
        kept.start()

    m = mask[...][None]
    sums = [convolve(field, half, taps.at[0], pair, width) for half in range(2)]
    lower, errors = [], []
    for part in range(2):
        preact = to_native(sums[0], sums[1], part, width)
        s = jax.nn.sigmoid(preact)
        shaped = (m * (preact * s)).astype(BF).astype(F32)
        slope = s * (1.0 + preact * (1.0 - s))
        out = (output_two[:, part].astype(F32) - shaped).astype(BF)
        restored[:, part] = out
        lower.append(out.astype(F32) * m)
        errors.append(m * (cotangent_two[:, part].astype(F32) * slope))
    write_parts(0, pair, lower, parts, depth)
    write_parts(1, pair, errors, parts, depth)

    @pl.when(pair == depth // 2 - 1)
    def _():
        kept.wait()


def second_kernel(depth, width, mask, taps_f, taps_g, centre, *refs):
    halos, (output_one, cotangent_one) = refs[:4], refs[4:6]
    restored, grad, parts = refs[6], refs[7], refs[8:13]
    field_l, field_e = refs[14], refs[15]
    kept = pltpu.make_async_copy(field_l, refs[13], refs[16])
    pair = pl.program_id(0)

    @pl.when(pair == 0)
    def _():
        build_field(field_l, 0, centre, halos, width)
        kept.start()
        build_field(field_e, 1, centre, halos, width)

    m = mask[...][None]
    sums = [convolve(field_l, half, taps_f.at[0], pair, width) for half in range(2)]
    spreads = [convolve(field_e, half, taps_g.at[0], pair, width) for half in range(2)]
    errors = []
    for part in range(2):
        preact = to_native(sums[0], sums[1], part, width)
        spread = to_native(spreads[0], spreads[1], part, width)
        s = jax.nn.sigmoid(preact)
        shaped = (m * (preact * s)).astype(BF).astype(F32)
        slope = s * (1.0 + preact * (1.0 - s))
        restored[:, part] = (output_one[:, part].astype(F32) - shaped).astype(BF)
        total = (cotangent_one[:, part].astype(F32) + m * spread).astype(BF)
        grad[:, part] = total
        errors.append(m * (total.astype(F32) * slope))
    write_parts(0, pair, errors, parts, depth)

    @pl.when(pair == depth // 2 - 1)
    def _():
        kept.wait()


def third_kernel(depth, width, mask, taps, centre, *refs):
    halos, cotangent_two, grad, field = refs[:4], refs[4], refs[5], refs[6]
    pair = pl.program_id(0)

    @pl.when(pair == 0)
    def _():
        build_field(field, 0, centre, halos, width)

    m = mask[...][None]
    sums = [convolve(field, half, taps.at[0], pair, width) for half in range(2)]
    for part in range(2):
        spread = to_native(sums[0], sums[1], part, width)
        grad[:, part] = (cotangent_two[:, part].astype(F32) + m * spread).astype(BF)


def conv_call(kernel, mask, matrices, centre, halos, natives, n_native_out, out_fields, fields, name):
    channels, depth, tall, width = natives[0].shape
    rows = channels * HALF
    length = matrices[0][0].shape[3]
    shapes = part_shapes(out_fields, channels, depth, width) if out_fields else []
    tap_specs = [
        pl.BlockSpec((1, 3, rows, length), functools.partial(lambda k, i: (k, 0, 0, 0), k)) for _, k in matrices
    ]
    native = natives[0].shape
    held = (2, length, (depth + 2) * width)
    export = 1 if out_fields else 0
    return pl.pallas_call(
        functools.partial(kernel, depth, width),
        out_shape=[jax.ShapeDtypeStruct(native, BF)] * n_native_out + [jax.ShapeDtypeStruct(s, BF) for s in shapes]
        + [jax.ShapeDtypeStruct(held, BF)] * export,
        grid=(depth // 2,),
        in_specs=[whole_spec(mask.shape)]
        + tap_specs
        + [whole_spec(centre.shape)]
        + [whole_spec(h.shape) for h in halos]
        + [pair_spec(native)] * len(natives),
        out_specs=[pair_spec(native)] * n_native_out
        + (part_specs(shapes, width) if shapes else [])
        + [pl.BlockSpec(memory_space=pl.ANY)] * export,
        scratch_shapes=[pltpu.VMEM(held, BF)] * fields + [pltpu.SemaphoreType.DMA] * export,
        compiler_params=params(),
        cost_estimate=cost(2 * 2 * rows * 3 * length * depth * width * fields, 2e7),
        name=name,
    )(mask, *[m for m, _ in matrices], centre, *halos, *natives)


def gradient_half_kernel(depth, width, field, errors, out):
    lanes = pl.ds(pl.multiple_of(pl.program_id(0) * width, width), depth * width)
    out[0] = lax.dot_general(
        errors[0, 0], field[0, :, lanes], (((1,), (1,)), ((), ())), preferred_element_type=F32
    )


def gradient_kernel(depth, width, field, errors, before, out, products):
    rows = errors.shape[2]
    channels = rows // HALF
    a = pl.program_id(0)
    lanes = pl.ds(pl.multiple_of(a * width, width), depth * width)

    products[...] = before[0] + lax.dot_general(
        errors[0, 0], field[0, :, lanes], (((1,), (1,)), ((), ())), preferred_element_type=F32
    )

    def pieces(value):
        high = value.astype(BF)
        return high, (value - high.astype(F32)).astype(BF)

    def tile(size):
        row = lax.broadcasted_iota(jnp.int32, (2 * HALF, size), 0) % HALF
        return row, lax.broadcasted_iota(jnp.int32, (2 * HALF, size), 1)

    gather_row = lax.broadcasted_iota(jnp.int32, (channels, rows), 0)
    gather_col = lax.broadcasted_iota(jnp.int32, (channels, rows), 1)
    gather = jnp.where(gather_col // HALF == gather_row, 1.0, 0.0).astype(BF)

    def chosen(parts, keep):
        total = None
        for part in parts:
            size = part.shape[1]
            kept = (part.reshape(rows // (2 * HALF), 2 * HALF, size) * keep[None]).reshape(rows, size)
            term = jnp.dot(gather, kept, preferred_element_type=F32)
            total = term if total is None else total + term
        return total

    row, col = tile(rows)
    bands = [jnp.where(col % HALF - row == b - 1, 1.0, 0.0).astype(BF) for b in range(3)]
    picked = {}
    for c in range(3):
        parts = pieces(products[:, c * rows : (c + 1) * rows])
        for b in range(3):
            picked[b, c] = chosen(parts, bands[b])
    row, col = tile(6 * channels)
    ends = jnp.where(row == jnp.where(col // channels % 2 == 0, 0, HALF - 1), 1.0, 0.0).astype(BF)
    sides = chosen(pieces(products[:, 3 * rows :]), ends)
    fold_row = lax.broadcasted_iota(jnp.int32, (rows, channels), 0)
    fold_col = lax.broadcasted_iota(jnp.int32, (rows, channels), 1)
    fold = jnp.where(fold_row // HALF == fold_col, 1.0, 0.0).astype(BF)
    summed = None
    for piece in pieces(jnp.concatenate([picked[b, c] for b in range(3) for c in range(3)], axis=0)):
        term = jnp.dot(piece, fold, preferred_element_type=F32)
        summed = term if summed is None else summed + term
    values = []
    for b in range(3):
        for c in range(3):
            at = (3 * b + c) * channels
            value = summed[at : at + channels]
            if b != 1:
                at = (2 * c + b // 2) * channels
                value = value + sides[:, at : at + channels]
            values.append(value)
    out[:, pl.ds(pl.multiple_of(a * 8 * channels, 8 * channels), 8 * channels)] = jnp.concatenate(values[:8], axis=1)
    empty = jnp.zeros((channels, channels), F32)
    tail = jnp.concatenate([jnp.where(a == k, values[8], empty) for k in range(3)] + [empty] * 5, axis=1)
    last = slice(24 * channels, 32 * channels)

    @pl.when(a == 0)
    def _():
        out[:, last] = tail

    @pl.when(a > 0)
    def _():
        out[:, last] = out[:, last] + tail


def weight_gradient(field, errors, which, half, width, before=None):
    _, length, columns = field.shape
    rows = errors.shape[2]
    channels = rows // HALF
    depth = errors.shape[3] // width
    raw = (3, rows, length)
    raw_spec = pl.BlockSpec((1, rows, length), lambda i: (i, 0, 0))
    last = before is not None
    result = (channels, 32 * channels) if last else raw
    return pl.pallas_call(
        functools.partial(gradient_kernel if last else gradient_half_kernel, depth, width),
        out_shape=jax.ShapeDtypeStruct(result, F32),
        grid=(3,),
        in_specs=[
            pl.BlockSpec((1, length, columns), lambda i: (half, 0, 0)),
            pl.BlockSpec((1, 1, rows, depth * width), lambda i: (which, half, 0, 0)),
        ]
        + [raw_spec] * last,
        out_specs=whole_spec(result) if last else raw_spec,
        scratch_shapes=[pltpu.VMEM((rows, length), F32)] * last,
        compiler_params=params(),
        cost_estimate=cost(2 * rows * 3 * length * depth * width, 1e7),
        name="weight_gradient",
    )(*([field, errors] + [before] * last))


def unpack_kernel(packed, *outs):
    channels = packed.shape[0]
    for k, out in enumerate(outs):
        for a in range(3):
            for t in range(9):
                at = 8 * a + t if t < 8 else 24 + a
                at = (32 * k + at) * channels
                out[9 * a + t] = packed[:, at : at + channels]


def unpack(packed):
    channels = packed.shape[0]
    shape = (27, channels, channels)
    return pl.pallas_call(
        unpack_kernel,
        out_shape=[jax.ShapeDtypeStruct(shape, F32)] * 2,
        grid=(1,),
        in_specs=[whole_spec(packed.shape)],
        out_specs=[whole_spec(shape)] * 2,
        compiler_params=params(),
        name="unpack",
    )(packed)


def total_over_devices(value, scale):
    axes = ("depth", "group")
    devices = lax.axis_size("depth") * lax.axis_size("group")
    shares = lax.all_to_all(value.reshape(devices, -1, 128), axes, 0, 0)
    share = jnp.sum(shares, axis=0) * scale
    everyone = lax.all_to_all(jnp.broadcast_to(share[None], shares.shape), axes, 0, 0)
    return everyone.reshape(value.shape)


def shift_along(value, axis, step):
    size = lax.axis_size(axis)
    return lax.ppermute(value, axis, [(i + step, i) for i in range(size) if 0 <= i + step < size])


def exchange_sides(faces):
    zlo, zhi, ylo, yhi = faces
    return shift_along(yhi, "group", -1), shift_along(ylo, "group", 1)


def exchange_faces(faces, sides, width):
    zlo, zhi, _, _ = faces
    low, high = sides
    first = jnp.concatenate([zlo, low[:, :, :width], high[:, :, :width]], axis=1)
    last = jnp.concatenate([zhi, low[:, :, -width:], high[:, :, -width:]], axis=1)
    return [shift_along(last, "depth", -1), shift_along(first, "depth", 1), low, high]


def after(value, others):
    return lax.optimization_barrier((value, others))[0]


def local(
    output_one, output_two, cotangent_one, cotangent_two, first_weight, second_weight, bricks
):
    brick_edge = output_one.shape[1]
    width = output_one.shape[3]
    slots = bricks.shape[2]
    groups = lax.axis_size("group")
    position = lax.axis_index("group")
    own_list = bricks[0][position]
    present = jnp.any(own_list[:, None] == jnp.arange(slots, dtype=jnp.int32)[None, :], axis=0)
    mask = jnp.repeat(present.astype(F32), brick_edge)[None, :]

    upper, *faces = upper_parts(output_one, mask)
    sides = exchange_sides(faces)

    def turned(kernel):
        return jnp.transpose(jnp.flip(kernel, 0), (0, 2, 1))

    taps_g = banded(jnp.stack([second_weight, turned(second_weight)]))
    sides = after(sides, taps_g)
    upper_halos = exchange_faces(faces, sides, width)
    taps_f = banded(jnp.stack([first_weight, turned(first_weight)]))
    upper = after(upper, taps_f)

    restored_two, middle, *faces, field = conv_call(
        first_kernel, mask, [(taps_g, 0)], upper, upper_halos, [output_two, cotangent_two], 1, 2, 1, "first_conv"
    )
    sides = exchange_sides(faces)
    second_a = weight_gradient(field, middle, 1, 0, width)
    sides = after(sides, second_a)
    middle_halos = exchange_faces(faces, sides, width)
    second_total = weight_gradient(field, middle, 1, 1, width, second_a)
    restored_one, input_grad_one, last, *faces, field = conv_call(
        second_kernel,
        mask,
        [(taps_f, 0), (taps_g, 1)],
        middle,
        middle_halos,
        [output_one, cotangent_one],
        2,
        1,
        2,
        "second_conv",
    )
    sides = exchange_sides(faces)
    first_a = weight_gradient(field, last, 0, 0, width)
    sides = after(sides, first_a)
    last_halos = exchange_faces(faces, sides, width)
    first_total = weight_gradient(field, last, 0, 1, width, first_a)
    (input_grad_two,) = conv_call(
        third_kernel, mask, [(taps_f, 1)], last, last_halos, [cotangent_two], 1, 0, 1, "third_conv"
    )
    scale = 1.0 / math.sqrt(
        float(brick_edge * lax.axis_size("depth") * output_one.shape[2] * groups * width)
    )
    packed = jnp.concatenate([first_total, second_total], axis=1)
    first_total, second_total = unpack(total_over_devices(packed, scale))
    return (restored_one, restored_two, input_grad_one, input_grad_two, first_total, second_total)


def solution(mesh):
    slab = P(None, "depth", "group", None)
    return jax.shard_map(
        local,
        mesh=mesh,
        in_specs=(slab, slab, slab, slab, P(), P(), P("depth", None, None)),
        out_specs=(slab, slab, slab, slab, P(), P()),
        check_vma=False,
    )
```

```python
import functools
import math

import jax
import jax.numpy as jnp
from jax import lax
from jax.experimental import pallas as pl
from jax.experimental.pallas import tpu as pltpu
from jax.sharding import PartitionSpec as P

BF = jnp.bfloat16
F32 = jnp.float32
HALF = 8


def shifted(plane, step):
    if step == 0:
        return plane
    width = plane.shape[1]
    lane = lax.broadcasted_iota(jnp.int32, plane.shape, 1)
    edge = 0 if step < 0 else width - 1
    rolled = pltpu.roll(plane, (-step) % width, axis=1)
    return jnp.where(lane == edge, jnp.zeros_like(rolled), rolled)


def picker(rows):
    channels = rows // HALF
    out = lax.broadcasted_iota(jnp.int32, (2 * channels, rows), 0)
    col = lax.broadcasted_iota(jnp.int32, (2 * channels, rows), 1)
    wanted = (out % channels) * HALF + jnp.where(out < channels, 0, HALF - 1)
    return jnp.where(col == wanted, 1.0, 0.0).astype(BF)


def build_field(field, f, centre, halos, width):
    zlo, zhi, ylo, yhi = halos
    rows = centre.shape[2]
    channels = rows // HALF
    depth = centre.shape[3] // width
    pick = picker(rows)
    side = 2 * channels
    plain = ((0, rows), (3 * rows, side))

    def unshifted(lanes, mains, low, high):
        for half in range(2):
            ends = jnp.dot(pick, mains[1 - half], preferred_element_type=F32).astype(BF)
            sides = [low, ends[:channels]] if half == 0 else [ends[channels:], high]
            field[half, rows : 2 * rows, lanes] = mains[half]
            field[half, 3 * rows + side : 3 * rows + 2 * side, lanes] = jnp.concatenate(sides, axis=0)

    for start, face in ((0, zlo), ((depth + 1) * width, zhi)):
        unshifted(
            slice(start, start + width),
            [face[f, 0:rows, :], face[f, rows : 2 * rows, :]],
            face[f, 2 * rows : 2 * rows + channels, :],
            face[f, 2 * rows + channels :, :],
        )
    unshifted(slice(width, (depth + 1) * width), [centre[f, 0], centre[f, 1]], ylo[f], yhi[f])

    def plane(number, carry):
        lanes = pl.ds(pl.multiple_of(number * width, width), width)
        for half in range(2):
            for start, size in plain:
                block = field[half, start + size : start + 2 * size, lanes]
                field[half, start : start + size, lanes] = shifted(block, -1)
                field[half, start + 2 * size : start + 3 * size, lanes] = shifted(block, 1)
        return carry

    lax.fori_loop(0, depth + 2, plane, 0, unroll=3)


def convolve(field, half, taps, pair, width):
    total = None
    for step in range(3):
        lanes = pl.ds(pl.multiple_of((2 * pair + step) * width, width), 2 * width)
        term = jnp.dot(taps[step], field[half, :, lanes], preferred_element_type=F32)
        total = term if total is None else total + term
    return total


def to_native(first, second, part, width):
    lanes = slice(part * width, (part + 1) * width)
    channels = first.shape[0] // HALF
    return jnp.concatenate(
        [first[:, lanes].reshape(channels, HALF, width), second[:, lanes].reshape(channels, HALF, width)], axis=1
    )


def write_parts(f, pair, planes, outs, depth):
    centre, zlo, zhi, ylo, yhi = outs
    channels, tall, width = planes[0].shape
    rows = channels * HALF
    lanes = pl.ds(pl.multiple_of(pair * 2 * width, width), 2 * width)
    pick = picker(rows)
    halves = []
    for half in range(2):
        block = jnp.concatenate(
            [p[:, half * HALF : (half + 1) * HALF, :].reshape(rows, width) for p in planes], axis=1
        ).astype(BF)
        centre[f, half] = block
        halves.append(block)
    low = jnp.dot(pick, halves[0], preferred_element_type=F32).astype(BF)[:channels]
    high = jnp.dot(pick, halves[1], preferred_element_type=F32).astype(BF)[channels:]
    ylo[f, :, lanes] = low
    yhi[f, :, lanes] = high

    @pl.when(pair == 0)
    def _():
        for half in range(2):
            zlo[f, half * rows : (half + 1) * rows, :] = halves[half][:, :width]

    @pl.when(pair == depth // 2 - 1)
    def _():
        for half in range(2):
            zhi[f, half * rows : (half + 1) * rows, :] = halves[half][:, width:]


def part_shapes(fields, channels, depth, width):
    rows = channels * HALF
    face = (fields, 2 * rows, width)
    side = (fields, channels, depth * width)
    return [(fields, 2, rows, depth * width), face, face, side, side]


def whole_spec(shape):
    return pl.BlockSpec(shape, lambda i: (0,) * len(shape))


def part_specs(shapes, width):
    fields, halves, rows, _ = shapes[0]
    centre = pl.BlockSpec((fields, halves, rows, 2 * width), lambda i: (0, 0, 0, i))
    return [centre] + [whole_spec(s) for s in shapes[1:]]


def pair_spec(shape):
    channels, _, tall, width = shape
    return pl.BlockSpec((channels, 2, tall, width), lambda i: (0, i, 0, 0))


def params(mebibytes):
    return pltpu.CompilerParams(dimension_semantics=("arbitrary",), vmem_limit_bytes=mebibytes * 1024 * 1024)


def cost(flops, nbytes):
    return pl.CostEstimate(flops=int(flops), bytes_accessed=int(nbytes), transcendentals=0)


def upper_kernel(depth, source, mask, *outs):
    pair = pl.program_id(0)
    m = mask[...][None]
    planes = [source[:, part].astype(F32) * m for part in range(2)]
    write_parts(0, pair, planes, outs, depth)


def upper_parts(source, mask):
    channels, depth, tall, width = source.shape
    shapes = part_shapes(1, channels, depth, width)
    return pl.pallas_call(
        functools.partial(upper_kernel, depth),
        out_shape=[jax.ShapeDtypeStruct(s, BF) for s in shapes],
        grid=(depth // 2,),
        in_specs=[pair_spec(source.shape), whole_spec(mask.shape)],
        out_specs=part_specs(shapes, width),
        compiler_params=params(16),
        cost_estimate=cost(1e8, 6e6),
        name="upper_parts",
    )(source, mask)


def taps_kernel(taps, out):
    channels = taps.shape[3]
    rows = channels * HALF
    chan = lax.broadcasted_iota(jnp.int32, (channels, rows), 0)
    col = lax.broadcasted_iota(jnp.int32, (channels, rows), 1)
    spread = jnp.where(col // HALF == chan, 1.0, 0.0).astype(BF)
    row_at = lax.broadcasted_iota(jnp.int32, (channels, HALF, rows), 1)
    col_at = lax.broadcasted_iota(jnp.int32, (channels, HALF, rows), 2) % HALF
    gap = col_at - row_at
    width = 6 * channels
    place_row = lax.broadcasted_iota(jnp.int32, (channels, width), 0)
    place_col = lax.broadcasted_iota(jnp.int32, (channels, width), 1)
    side_row = lax.broadcasted_iota(jnp.int32, (channels, HALF, width), 1)
    side_lane = lax.broadcasted_iota(jnp.int32, (channels, HALF, width), 2) // channels % 2
    keep = ((side_row == 0) & (side_lane == 0)) | ((side_row == HALF - 1) & (side_lane == 1))
    for a in range(3):
        for c in range(3):
            wide = [
                jnp.dot(taps[0, 9 * a + 3 * b + c], spread, preferred_element_type=F32)[:, None, :] for b in range(3)
            ]
            block = jnp.where(gap == 0, wide[1], 0.0)
            block = jnp.where(gap == -1, wide[0], block)
            block = jnp.where(gap == 1, wide[2], block)
            out[0, a, :, c * rows : (c + 1) * rows] = block.reshape(rows, rows).astype(BF)
        edge = None
        for c in range(3):
            for end in range(2):
                place = jnp.where(place_col == (2 * c + end) * channels + place_row, 1.0, 0.0).astype(BF)
                term = jnp.dot(taps[0, 9 * a + 6 * end + c], place, preferred_element_type=F32)
                edge = term if edge is None else edge + term
        edge = jnp.where(keep, edge[:, None, :], 0.0)
        out[0, a, :, 3 * rows :] = edge.reshape(rows, width).astype(BF)


def banded(kernels):
    count, taps, channels, _ = kernels.shape
    rows = channels * HALF
    length = 3 * rows + 6 * channels
    return pl.pallas_call(
        taps_kernel,
        out_shape=jax.ShapeDtypeStruct((count, 3, rows, length), BF),
        grid=(count,),
        in_specs=[
            pl.BlockSpec((1, taps, channels, channels), lambda i: (i, 0, 0, 0)),
        ],
        out_specs=pl.BlockSpec((1, 3, rows, length), lambda i: (i, 0, 0, 0)),
        compiler_params=params(16),
        cost_estimate=cost(1e9, 8e6),
        name="banded_taps",
    )(kernels)


def first_kernel(depth, width, mask, taps, centre, *refs):
    halos, (output_two, cotangent_two), restored, parts, field = refs[:4], refs[4:6], refs[6], refs[7:12], refs[13]
    pair = pl.program_id(0)
    kept = pltpu.make_async_copy(field, refs[12], refs[14])

    @pl.when(pair == 0)
    def _():
        build_field(field, 0, centre, halos, width)
        kept.start()

    m = mask[...][None]
    sums = [convolve(field, half, taps.at[0], pair, width) for half in range(2)]
    lower, errors = [], []
    for part in range(2):
        preact = to_native(sums[0], sums[1], part, width)
        s = jax.nn.sigmoid(preact)
        inside = m * s
        silu = preact * inside
        shaped = silu.astype(BF).astype(F32)
        slope = inside + silu * (1.0 - s)
        out = (output_two[:, part].astype(F32) - shaped).astype(BF)
        restored[:, part] = out
        lower.append(out.astype(F32) * m)
        errors.append(cotangent_two[:, part].astype(F32) * slope)
    write_parts(0, pair, lower, parts, depth)
    write_parts(1, pair, errors, parts, depth)

    @pl.when(pair == depth // 2 - 1)
    def _():
        kept.wait()


def second_kernel(depth, width, mask, taps_f, taps_g, centre, *refs):
    halos, (output_one, cotangent_one) = refs[:4], refs[4:6]
    restored, grad, parts = refs[6], refs[7], refs[8:13]
    field_l, field_e = refs[14], refs[15]
    kept = pltpu.make_async_copy(field_l, refs[13], refs[16])
    pair = pl.program_id(0)

    @pl.when(pair == 0)
    def _():
        build_field(field_l, 0, centre, halos, width)
        kept.start()
        build_field(field_e, 1, centre, halos, width)

    m = mask[...][None]
    sums = [convolve(field_l, half, taps_f.at[0], pair, width) for half in range(2)]
    spreads = [convolve(field_e, half, taps_g.at[0], pair, width) for half in range(2)]
    errors = []
    for part in range(2):
        preact = to_native(sums[0], sums[1], part, width)
        spread = to_native(spreads[0], spreads[1], part, width)
        s = jax.nn.sigmoid(preact)
        inside = m * s
        silu = preact * inside
        shaped = silu.astype(BF).astype(F32)
        slope = inside + silu * (1.0 - s)
        restored[:, part] = (output_one[:, part].astype(F32) - shaped).astype(BF)
        total = (cotangent_one[:, part].astype(F32) + m * spread).astype(BF)
        grad[:, part] = total
        errors.append(total.astype(F32) * slope)
    write_parts(0, pair, errors, parts, depth)

    @pl.when(pair == depth // 2 - 1)
    def _():
        kept.wait()


def third_kernel(depth, width, mask, taps, centre, *refs):
    halos, cotangent_two, grad, field = refs[:4], refs[4], refs[5], refs[6]
    pair = pl.program_id(0)

    @pl.when(pair == 0)
    def _():
        build_field(field, 0, centre, halos, width)

    m = mask[...][None]
    sums = [convolve(field, half, taps.at[0], pair, width) for half in range(2)]
    for part in range(2):
        spread = to_native(sums[0], sums[1], part, width)
        grad[:, part] = (cotangent_two[:, part].astype(F32) + m * spread).astype(BF)


def conv_call(kernel, mask, matrices, centre, halos, natives, n_native_out, out_fields, fields, name):
    channels, depth, tall, width = natives[0].shape
    rows = channels * HALF
    length = matrices[0][0].shape[3]
    shapes = part_shapes(out_fields, channels, depth, width) if out_fields else []
    tap_specs = [
        pl.BlockSpec((1, 3, rows, length), functools.partial(lambda k, i: (k, 0, 0, 0), k)) for _, k in matrices
    ]
    native = natives[0].shape
    held = (2, length, (depth + 2) * width)
    export = 1 if out_fields else 0
    return pl.pallas_call(
        functools.partial(kernel, depth, width),
        out_shape=[jax.ShapeDtypeStruct(native, BF)] * n_native_out + [jax.ShapeDtypeStruct(s, BF) for s in shapes]
        + [jax.ShapeDtypeStruct(held, BF)] * export,
        grid=(depth // 2,),
        in_specs=[whole_spec(mask.shape)]
        + tap_specs
        + [whole_spec(centre.shape)]
        + [whole_spec(h.shape) for h in halos]
        + [pair_spec(native)] * len(natives),
        out_specs=[pair_spec(native)] * n_native_out
        + (part_specs(shapes, width) if shapes else [])
        + [pl.BlockSpec(memory_space=pl.ANY)] * export,
        scratch_shapes=[pltpu.VMEM(held, BF)] * fields + [pltpu.SemaphoreType.DMA] * export,
        compiler_params=params(28 + 16 * (fields - 1)),
        cost_estimate=cost(2 * 2 * rows * 3 * length * depth * width * fields, 2e7),
        name=name,
    )(mask, *[m for m, _ in matrices], centre, *halos, *natives)


def gradient_half_kernel(depth, width, field, errors, out):
    lanes = pl.ds(pl.multiple_of(pl.program_id(0) * width, width), depth * width)
    out[0] = lax.dot_general(
        errors[0, 0], field[0, :, lanes], (((1,), (1,)), ((), ())), preferred_element_type=F32
    )


def gradient_kernel(depth, width, field, errors, before, out, products):
    rows = errors.shape[2]
    channels = rows // HALF
    a = pl.program_id(0)
    lanes = pl.ds(pl.multiple_of(a * width, width), depth * width)

    products[...] = before[0] + lax.dot_general(
        errors[0, 0], field[0, :, lanes], (((1,), (1,)), ((), ())), preferred_element_type=F32
    )

    def pieces(value):
        high = value.astype(BF)
        return high, (value - high.astype(F32)).astype(BF)

    def tile(size):
        row = lax.broadcasted_iota(jnp.int32, (2 * HALF, size), 0) % HALF
        return row, lax.broadcasted_iota(jnp.int32, (2 * HALF, size), 1)

    gather_row = lax.broadcasted_iota(jnp.int32, (channels, rows), 0)
    gather_col = lax.broadcasted_iota(jnp.int32, (channels, rows), 1)
    gather = jnp.where(gather_col // HALF == gather_row, 1.0, 0.0).astype(BF)

    def chosen(parts, keep):
        total = None
        for part in parts:
            size = part.shape[1]
            kept = (part.reshape(rows // (2 * HALF), 2 * HALF, size) * keep[None]).reshape(rows, size)
            term = jnp.dot(gather, kept, preferred_element_type=F32)
            total = term if total is None else total + term
        return total

    row, col = tile(rows)
    bands = [jnp.where(col % HALF - row == b - 1, 1.0, 0.0).astype(BF) for b in range(3)]
    picked = {}
    for c in range(3):
        parts = pieces(products[:, c * rows : (c + 1) * rows])
        for b in range(3):
            picked[b, c] = chosen(parts, bands[b])
    row, col = tile(6 * channels)
    ends = jnp.where(row == jnp.where(col // channels % 2 == 0, 0, HALF - 1), 1.0, 0.0).astype(BF)
    sides = chosen(pieces(products[:, 3 * rows :]), ends)
    fold_row = lax.broadcasted_iota(jnp.int32, (rows, channels), 0)
    fold_col = lax.broadcasted_iota(jnp.int32, (rows, channels), 1)
    fold = jnp.where(fold_row // HALF == fold_col, 1.0, 0.0).astype(BF)
    summed = None
    for piece in pieces(jnp.concatenate([picked[b, c] for b in range(3) for c in range(3)], axis=0)):
        term = jnp.dot(piece, fold, preferred_element_type=F32)
        summed = term if summed is None else summed + term
    values = []
    for b in range(3):
        for c in range(3):
            at = (3 * b + c) * channels
            value = summed[at : at + channels]
            if b != 1:
                at = (2 * c + b // 2) * channels
                value = value + sides[:, at : at + channels]
            values.append(value)
    out[:, pl.ds(pl.multiple_of(a * 8 * channels, 8 * channels), 8 * channels)] = jnp.concatenate(values[:8], axis=1)
    empty = jnp.zeros((channels, channels), F32)
    tail = jnp.concatenate([jnp.where(a == k, values[8], empty) for k in range(3)] + [empty] * 5, axis=1)
    last = slice(24 * channels, 32 * channels)

    @pl.when(a == 0)
    def _():
        out[:, last] = tail

    @pl.when(a > 0)
    def _():
        out[:, last] = out[:, last] + tail


def weight_gradient(field, errors, which, half, width, before=None):
    _, length, columns = field.shape
    rows = errors.shape[2]
    channels = rows // HALF
    depth = errors.shape[3] // width
    raw = (3, rows, length)
    raw_spec = pl.BlockSpec((1, rows, length), lambda i: (i, 0, 0))
    last = before is not None
    result = (channels, 32 * channels) if last else raw
    return pl.pallas_call(
        functools.partial(gradient_kernel if last else gradient_half_kernel, depth, width),
        out_shape=jax.ShapeDtypeStruct(result, F32),
        grid=(3,),
        in_specs=[
            pl.BlockSpec((1, length, columns), lambda i: (half, 0, 0)),
            pl.BlockSpec((1, 1, rows, depth * width), lambda i: (which, half, 0, 0)),
        ]
        + [raw_spec] * last,
        out_specs=whole_spec(result) if last else raw_spec,
        scratch_shapes=[pltpu.VMEM((rows, length), F32)] * last,
        compiler_params=params(24),
        cost_estimate=cost(2 * rows * 3 * length * depth * width, 1e7),
        name="weight_gradient",
    )(*([field, errors] + [before] * last))


def unpack_kernel(packed, *outs):
    channels = packed.shape[0]
    fit = 128 // channels
    for k, out in enumerate(outs):
        for a in range(3):
            for t in range(9):
                at = 8 * a + t if t < 8 else 24 + a
                at += 32 * k
                lane = at % fit * channels
                out[9 * a + t] = packed[:, at // fit, lane : lane + channels]


def unpack(packed):
    channels = packed.shape[0]
    shape = (27, channels, channels)
    return pl.pallas_call(
        unpack_kernel,
        out_shape=[jax.ShapeDtypeStruct(shape, F32)] * 2,
        grid=(1,),
        in_specs=[whole_spec(packed.shape)],
        out_specs=[whole_spec(shape)] * 2,
        compiler_params=params(16),
        name="unpack",
    )(packed)


def total_over_devices(value, scale):
    axes = ("depth", "group")
    devices = lax.axis_size("depth") * lax.axis_size("group")
    shares = lax.all_to_all(value.reshape(devices, -1, 128), axes, 0, 0)
    share = jnp.sum(shares, axis=0) * scale
    everyone = lax.all_to_all(jnp.broadcast_to(share[None], shares.shape), axes, 0, 0)
    return everyone


def shift_along(value, axis, step):
    size = lax.axis_size(axis)
    return lax.ppermute(value, axis, [(i + step, i) for i in range(size) if 0 <= i + step < size])


def exchange_sides(faces):
    zlo, zhi, ylo, yhi = faces
    return shift_along(yhi, "group", -1), shift_along(ylo, "group", 1)


def exchange_faces(faces, sides, width):
    zlo, zhi, _, _ = faces
    low, high = sides
    first = jnp.concatenate([zlo, low[:, :, :width], high[:, :, :width]], axis=1)
    last = jnp.concatenate([zhi, low[:, :, -width:], high[:, :, -width:]], axis=1)
    return [shift_along(last, "depth", -1), shift_along(first, "depth", 1), low, high]


def after(value, others):
    return lax.optimization_barrier((value, others))[0]


def local(
    output_one, output_two, cotangent_one, cotangent_two, first_weight, second_weight, bricks
):
    brick_edge = output_one.shape[1]
    width = output_one.shape[3]
    slots = bricks.shape[2]
    groups = lax.axis_size("group")
    position = lax.axis_index("group")
    own_list = bricks[0][position]
    present = jnp.any(own_list[:, None] == jnp.arange(slots, dtype=jnp.int32)[None, :], axis=0)
    mask = jnp.repeat(present.astype(F32), brick_edge)[None, :]

    upper, *faces = upper_parts(output_one, mask)
    sides = exchange_sides(faces)

    def turned(kernel):
        return jnp.transpose(jnp.flip(kernel, 0), (0, 2, 1))

    taps_g = banded(jnp.stack([second_weight, turned(second_weight)]))
    sides = after(sides, taps_g)
    upper_halos = exchange_faces(faces, sides, width)
    taps_f = banded(jnp.stack([first_weight, turned(first_weight)]))
    upper = after(upper, taps_f)

    restored_two, middle, *faces, field = conv_call(
        first_kernel, mask, [(taps_g, 0)], upper, upper_halos, [output_two, cotangent_two], 1, 2, 1, "first_conv"
    )
    sides = exchange_sides(faces)
    second_a = weight_gradient(field, middle, 1, 0, width)
    sides = after(sides, second_a)
    middle_halos = exchange_faces(faces, sides, width)
    second_total = weight_gradient(field, middle, 1, 1, width, second_a)
    restored_one, input_grad_one, last, *faces, field = conv_call(
        second_kernel,
        mask,
        [(taps_f, 0), (taps_g, 1)],
        middle,
        middle_halos,
        [output_one, cotangent_one],
        2,
        1,
        2,
        "second_conv",
    )
    sides = exchange_sides(faces)
    first_a = weight_gradient(field, last, 0, 0, width)
    sides = after(sides, first_a)
    last_halos = exchange_faces(faces, sides, width)
    first_total = weight_gradient(field, last, 0, 1, width, first_a)
    (input_grad_two,) = conv_call(
        third_kernel, mask, [(taps_f, 1)], last, last_halos, [cotangent_two], 1, 0, 1, "third_conv"
    )
    scale = 1.0 / math.sqrt(
        float(brick_edge * lax.axis_size("depth") * output_one.shape[2] * groups * width)
    )
    packed = jnp.concatenate([first_total, second_total], axis=1)
    first_total, second_total = unpack(total_over_devices(packed, scale).reshape(packed.shape[0], -1, 128))
    return (restored_one, restored_two, input_grad_one, input_grad_two, first_total, second_total)


def solution(mesh):
    slab = P(None, "depth", "group", None)
    return jax.shard_map(
        local,
        mesh=mesh,
        in_specs=(slab, slab, slab, slab, P(), P(), P("depth", None, None)),
        out_specs=(slab, slab, slab, slab, P(), P()),
        check_vma=False,
    )
```

```python
import functools
import math

import jax
import jax.numpy as jnp
from jax import lax
from jax.experimental import pallas as pl
from jax.experimental.pallas import tpu as pltpu
from jax.sharding import PartitionSpec as P

BF = jnp.bfloat16
F32 = jnp.float32
HALF = 8


def shifted(plane, step):
    if step == 0:
        return plane
    width = plane.shape[1]
    lane = lax.broadcasted_iota(jnp.int32, plane.shape, 1)
    edge = 0 if step < 0 else width - 1
    rolled = pltpu.roll(plane, (-step) % width, axis=1)
    return jnp.where(lane == edge, jnp.zeros_like(rolled), rolled)


def picker(rows):
    channels = rows // HALF
    out = lax.broadcasted_iota(jnp.int32, (2 * channels, rows), 0)
    col = lax.broadcasted_iota(jnp.int32, (2 * channels, rows), 1)
    wanted = (out % channels) * HALF + jnp.where(out < channels, 0, HALF - 1)
    return jnp.where(col == wanted, 1.0, 0.0).astype(BF)


def build_field(field, f, centre, halos, width):
    zlo, zhi, ylo, yhi = halos
    rows = centre.shape[2]
    channels = rows // HALF
    depth = centre.shape[3] // width
    pick = picker(rows)
    side = 2 * channels
    plain = ((0, rows), (3 * rows, side))

    def unshifted(lanes, mains, low, high):
        for half in range(2):
            ends = jnp.dot(pick, mains[1 - half], preferred_element_type=F32).astype(BF)
            sides = [low, ends[:channels]] if half == 0 else [ends[channels:], high]
            field[half, rows : 2 * rows, lanes] = mains[half]
            field[half, 3 * rows + side : 3 * rows + 2 * side, lanes] = jnp.concatenate(sides, axis=0)

    for start, face in ((0, zlo), ((depth + 1) * width, zhi)):
        unshifted(
            slice(start, start + width),
            [face[f, 0:rows, :], face[f, rows : 2 * rows, :]],
            face[f, 2 * rows : 2 * rows + channels, :],
            face[f, 2 * rows + channels :, :],
        )
    unshifted(slice(width, (depth + 1) * width), [centre[f, 0], centre[f, 1]], ylo[f], yhi[f])

    def plane(number, carry):
        lanes = pl.ds(pl.multiple_of(number * width, width), width)
        for half in range(2):
            for start, size in plain:
                block = field[half, start + size : start + 2 * size, lanes]
                field[half, start : start + size, lanes] = shifted(block, -1)
                field[half, start + 2 * size : start + 3 * size, lanes] = shifted(block, 1)
        return carry

    lax.fori_loop(0, depth + 2, plane, 0, unroll=3)


def convolve(field, half, taps, pair, width):
    total = None
    for step in range(3):
        lanes = pl.ds(pl.multiple_of((2 * pair + step) * width, width), 2 * width)
        term = jnp.dot(taps[step], field[half, :, lanes], preferred_element_type=F32)
        total = term if total is None else total + term
    return total


def to_native(first, second, part, width):
    lanes = slice(part * width, (part + 1) * width)
    channels = first.shape[0] // HALF
    return jnp.concatenate(
        [first[:, lanes].reshape(channels, HALF, width), second[:, lanes].reshape(channels, HALF, width)], axis=1
    )


def write_parts(f, pair, planes, outs, depth):
    centre, zlo, zhi, ylo, yhi = outs
    channels, tall, width = planes[0].shape
    rows = channels * HALF
    lanes = pl.ds(pl.multiple_of(pair * 2 * width, width), 2 * width)
    pick = picker(rows)
    halves = []
    for half in range(2):
        block = jnp.concatenate(
            [p[:, half * HALF : (half + 1) * HALF, :].reshape(rows, width) for p in planes], axis=1
        ).astype(BF)
        centre[f, half] = block
        halves.append(block)
    low = jnp.dot(pick, halves[0], preferred_element_type=F32).astype(BF)[:channels]
    high = jnp.dot(pick, halves[1], preferred_element_type=F32).astype(BF)[channels:]
    ylo[f, :, lanes] = low
    yhi[f, :, lanes] = high

    @pl.when(pair == 0)
    def _():
        for half in range(2):
            zlo[f, half * rows : (half + 1) * rows, :] = halves[half][:, :width]

    @pl.when(pair == depth // 2 - 1)
    def _():
        for half in range(2):
            zhi[f, half * rows : (half + 1) * rows, :] = halves[half][:, width:]


def part_shapes(fields, channels, depth, width):
    rows = channels * HALF
    face = (fields, 2 * rows, width)
    side = (fields, channels, depth * width)
    return [(fields, 2, rows, depth * width), face, face, side, side]


def whole_spec(shape):
    return pl.BlockSpec(shape, lambda i: (0,) * len(shape))


def part_specs(shapes, width):
    fields, halves, rows, _ = shapes[0]
    centre = pl.BlockSpec((fields, halves, rows, 2 * width), lambda i: (0, 0, 0, i))
    return [centre] + [whole_spec(s) for s in shapes[1:]]


def fixed_spec(shape, index=None):
    index = index or (0,) * len(shape)
    return pl.BlockSpec(shape, lambda i: index, pipeline_mode=pl.Buffered(1))


def pair_spec(shape):
    channels, _, tall, width = shape
    return pl.BlockSpec((channels, 2, tall, width), lambda i: (0, i, 0, 0))


def params(mebibytes):
    return pltpu.CompilerParams(dimension_semantics=("arbitrary",), vmem_limit_bytes=mebibytes * 1024 * 1024)


def streamed(value):
    return pltpu.with_memory_space_constraint(value, pltpu.HBM)


def cost(flops, nbytes):
    return pl.CostEstimate(flops=int(flops), bytes_accessed=int(nbytes), transcendentals=0)


def upper_kernel(depth, source, mask, *outs):
    pair = pl.program_id(0)
    m = mask[...][None]
    planes = [source[:, part].astype(F32) * m for part in range(2)]
    write_parts(0, pair, planes, outs, depth)


def upper_parts(source, mask):
    channels, depth, tall, width = source.shape
    shapes = part_shapes(1, channels, depth, width)
    return pl.pallas_call(
        functools.partial(upper_kernel, depth),
        out_shape=[jax.ShapeDtypeStruct(s, BF) for s in shapes],
        grid=(depth // 2,),
        in_specs=[pair_spec(source.shape), whole_spec(mask.shape)],
        out_specs=part_specs(shapes, width),
        compiler_params=params(16),
        cost_estimate=cost(1e8, 6e6),
        name="upper_parts",
    )(source, mask)


def taps_kernel(taps, out):
    channels = taps.shape[3]
    rows = channels * HALF
    chan = lax.broadcasted_iota(jnp.int32, (channels, rows), 0)
    col = lax.broadcasted_iota(jnp.int32, (channels, rows), 1)
    spread = jnp.where(col // HALF == chan, 1.0, 0.0).astype(BF)
    row_at = lax.broadcasted_iota(jnp.int32, (channels, HALF, rows), 1)
    col_at = lax.broadcasted_iota(jnp.int32, (channels, HALF, rows), 2) % HALF
    gap = col_at - row_at
    width = 6 * channels
    place_row = lax.broadcasted_iota(jnp.int32, (channels, width), 0)
    place_col = lax.broadcasted_iota(jnp.int32, (channels, width), 1)
    side_row = lax.broadcasted_iota(jnp.int32, (channels, HALF, width), 1)
    side_lane = lax.broadcasted_iota(jnp.int32, (channels, HALF, width), 2) // channels % 2
    keep = ((side_row == 0) & (side_lane == 0)) | ((side_row == HALF - 1) & (side_lane == 1))
    for a in range(3):
        for c in range(3):
            wide = [
                jnp.dot(taps[0, 9 * a + 3 * b + c], spread, preferred_element_type=F32)[:, None, :] for b in range(3)
            ]
            block = jnp.where(gap == 0, wide[1], 0.0)
            block = jnp.where(gap == -1, wide[0], block)
            block = jnp.where(gap == 1, wide[2], block)
            out[0, a, :, c * rows : (c + 1) * rows] = block.reshape(rows, rows).astype(BF)
        edge = None
        for c in range(3):
            for end in range(2):
                place = jnp.where(place_col == (2 * c + end) * channels + place_row, 1.0, 0.0).astype(BF)
                term = jnp.dot(taps[0, 9 * a + 6 * end + c], place, preferred_element_type=F32)
                edge = term if edge is None else edge + term
        edge = jnp.where(keep, edge[:, None, :], 0.0)
        out[0, a, :, 3 * rows :] = edge.reshape(rows, width).astype(BF)


def banded(kernels):
    count, taps, channels, _ = kernels.shape
    rows = channels * HALF
    length = 3 * rows + 6 * channels
    return pl.pallas_call(
        taps_kernel,
        out_shape=jax.ShapeDtypeStruct((count, 3, rows, length), BF),
        grid=(count,),
        in_specs=[
            pl.BlockSpec((1, taps, channels, channels), lambda i: (i, 0, 0, 0)),
        ],
        out_specs=pl.BlockSpec((1, 3, rows, length), lambda i: (i, 0, 0, 0)),
        compiler_params=params(16),
        cost_estimate=cost(1e9, 8e6),
        name="banded_taps",
    )(kernels)


def first_kernel(depth, width, mask, taps, centre, *refs):
    halos, (output_two, cotangent_two), restored, parts, field = refs[:4], refs[4:6], refs[6], refs[7:12], refs[13]
    pair = pl.program_id(0)
    kept = pltpu.make_async_copy(field, refs[12], refs[14])

    @pl.when(pair == 0)
    def _():
        build_field(field, 0, centre, halos, width)
        kept.start()

    m = mask[...][None]
    sums = [convolve(field, half, taps.at[0], pair, width) for half in range(2)]
    lower, errors = [], []
    for part in range(2):
        preact = to_native(sums[0], sums[1], part, width)
        s = jax.nn.sigmoid(preact)
        inside = m * s
        silu = preact * inside
        shaped = silu.astype(BF).astype(F32)
        slope = inside + silu * (1.0 - s)
        out = (output_two[:, part].astype(F32) - shaped).astype(BF)
        restored[:, part] = out
        lower.append(out.astype(F32) * m)
        errors.append(cotangent_two[:, part].astype(F32) * slope)
    write_parts(0, pair, lower, parts, depth)
    write_parts(1, pair, errors, parts, depth)

    @pl.when(pair == depth // 2 - 1)
    def _():
        kept.wait()


def second_kernel(depth, width, mask, taps_f, taps_g, centre, *refs):
    halos, (output_one, cotangent_one) = refs[:4], refs[4:6]
    restored, grad, parts = refs[6], refs[7], refs[8:13]
    field_l, field_e = refs[14], refs[15]
    kept = pltpu.make_async_copy(field_l, refs[13], refs[16])
    pair = pl.program_id(0)

    @pl.when(pair == 0)
    def _():
        build_field(field_l, 0, centre, halos, width)
        kept.start()
        build_field(field_e, 1, centre, halos, width)

    m = mask[...][None]
    sums = [convolve(field_l, half, taps_f.at[0], pair, width) for half in range(2)]
    spreads = [convolve(field_e, half, taps_g.at[0], pair, width) for half in range(2)]
    errors = []
    for part in range(2):
        preact = to_native(sums[0], sums[1], part, width)
        spread = to_native(spreads[0], spreads[1], part, width)
        s = jax.nn.sigmoid(preact)
        inside = m * s
        silu = preact * inside
        shaped = silu.astype(BF).astype(F32)
        slope = inside + silu * (1.0 - s)
        restored[:, part] = (output_one[:, part].astype(F32) - shaped).astype(BF)
        total = (cotangent_one[:, part].astype(F32) + m * spread).astype(BF)
        grad[:, part] = total
        errors.append(total.astype(F32) * slope)
    write_parts(0, pair, errors, parts, depth)

    @pl.when(pair == depth // 2 - 1)
    def _():
        kept.wait()


def third_kernel(depth, width, mask, taps, centre, *refs):
    halos, cotangent_two, grad, field = refs[:4], refs[4], refs[5], refs[6]
    pair = pl.program_id(0)

    @pl.when(pair == 0)
    def _():
        build_field(field, 0, centre, halos, width)

    m = mask[...][None]
    sums = [convolve(field, half, taps.at[0], pair, width) for half in range(2)]
    for part in range(2):
        spread = to_native(sums[0], sums[1], part, width)
        grad[:, part] = (cotangent_two[:, part].astype(F32) + m * spread).astype(BF)


def conv_call(kernel, mask, matrices, centre, halos, natives, n_native_out, out_fields, fields, name):
    channels, depth, tall, width = natives[0].shape
    rows = channels * HALF
    length = matrices[0][0].shape[3]
    shapes = part_shapes(out_fields, channels, depth, width) if out_fields else []
    tap_specs = [
        fixed_spec((1, 3, rows, length), (k, 0, 0, 0)) for _, k in matrices
    ]
    native = natives[0].shape
    held = (2, length, (depth + 2) * width)
    export = 1 if out_fields else 0
    return pl.pallas_call(
        functools.partial(kernel, depth, width),
        out_shape=[jax.ShapeDtypeStruct(native, BF)] * n_native_out + [jax.ShapeDtypeStruct(s, BF) for s in shapes]
        + [jax.ShapeDtypeStruct(held, BF)] * export,
        grid=(depth // 2,),
        in_specs=[fixed_spec(mask.shape)]
        + tap_specs
        + [fixed_spec(centre.shape)]
        + [fixed_spec(h.shape) for h in halos]
        + [pair_spec(native)] * len(natives),
        out_specs=[pair_spec(native)] * n_native_out
        + (part_specs(shapes, width) if shapes else [])
        + [pl.BlockSpec(memory_space=pl.ANY)] * export,
        scratch_shapes=[pltpu.VMEM(held, BF)] * fields + [pltpu.SemaphoreType.DMA] * export,
        compiler_params=params(22 + 12 * (fields - 1)),
        cost_estimate=cost(2 * 2 * rows * 3 * length * depth * width * fields, 2e7),
        name=name,
    )(mask, *[streamed(m) for m, _ in matrices], centre, *halos, *[streamed(v) for v in natives])


def gradient_half_kernel(depth, width, field, errors, out):
    lanes = pl.ds(pl.multiple_of(pl.program_id(0) * width, width), depth * width)
    out[0] = lax.dot_general(
        errors[0, 0], field[0, :, lanes], (((1,), (1,)), ((), ())), preferred_element_type=F32
    )


def gradient_kernel(depth, width, field, errors, before, out, products):
    rows = errors.shape[2]
    channels = rows // HALF
    a = pl.program_id(0)
    lanes = pl.ds(pl.multiple_of(a * width, width), depth * width)

    products[...] = before[0] + lax.dot_general(
        errors[0, 0], field[0, :, lanes], (((1,), (1,)), ((), ())), preferred_element_type=F32
    )

    def pieces(value):
        high = value.astype(BF)
        return high, (value - high.astype(F32)).astype(BF)

    def tile(size):
        row = lax.broadcasted_iota(jnp.int32, (2 * HALF, size), 0) % HALF
        return row, lax.broadcasted_iota(jnp.int32, (2 * HALF, size), 1)

    gather_row = lax.broadcasted_iota(jnp.int32, (channels, rows), 0)
    gather_col = lax.broadcasted_iota(jnp.int32, (channels, rows), 1)
    gather = jnp.where(gather_col // HALF == gather_row, 1.0, 0.0).astype(BF)

    def chosen(parts, keep):
        total = None
        for part in parts:
            size = part.shape[1]
            kept = (part.reshape(rows // (2 * HALF), 2 * HALF, size) * keep[None]).reshape(rows, size)
            term = jnp.dot(gather, kept, preferred_element_type=F32)
            total = term if total is None else total + term
        return total

    row, col = tile(rows)
    bands = [jnp.where(col % HALF - row == b - 1, 1.0, 0.0).astype(BF) for b in range(3)]
    picked = {}
    for c in range(3):
        parts = pieces(products[:, c * rows : (c + 1) * rows])
        for b in range(3):
            picked[b, c] = chosen(parts, bands[b])
    row, col = tile(6 * channels)
    ends = jnp.where(row == jnp.where(col // channels % 2 == 0, 0, HALF - 1), 1.0, 0.0).astype(BF)
    sides = chosen(pieces(products[:, 3 * rows :]), ends)
    fold_row = lax.broadcasted_iota(jnp.int32, (rows, channels), 0)
    fold_col = lax.broadcasted_iota(jnp.int32, (rows, channels), 1)
    fold = jnp.where(fold_row // HALF == fold_col, 1.0, 0.0).astype(BF)
    summed = None
    for piece in pieces(jnp.concatenate([picked[b, c] for b in range(3) for c in range(3)], axis=0)):
        term = jnp.dot(piece, fold, preferred_element_type=F32)
        summed = term if summed is None else summed + term
    values = []
    for b in range(3):
        for c in range(3):
            at = (3 * b + c) * channels
            value = summed[at : at + channels]
            if b != 1:
                at = (2 * c + b // 2) * channels
                value = value + sides[:, at : at + channels]
            values.append(value)
    out[:, pl.ds(pl.multiple_of(a * 8 * channels, 8 * channels), 8 * channels)] = jnp.concatenate(values[:8], axis=1)
    empty = jnp.zeros((channels, channels), F32)
    tail = jnp.concatenate([jnp.where(a == k, values[8], empty) for k in range(3)] + [empty] * 5, axis=1)
    last = slice(24 * channels, 32 * channels)

    @pl.when(a == 0)
    def _():
        out[:, last] = tail

    @pl.when(a > 0)
    def _():
        out[:, last] = out[:, last] + tail


def weight_gradient(field, errors, which, half, width, before=None):
    _, length, columns = field.shape
    rows = errors.shape[2]
    channels = rows // HALF
    depth = errors.shape[3] // width
    raw = (3, rows, length)
    raw_spec = pl.BlockSpec((1, rows, length), lambda i: (i, 0, 0))
    last = before is not None
    result = (channels, 32 * channels) if last else raw
    return pl.pallas_call(
        functools.partial(gradient_kernel if last else gradient_half_kernel, depth, width),
        out_shape=jax.ShapeDtypeStruct(result, F32),
        grid=(3,),
        in_specs=[
            fixed_spec((1, length, columns), (half, 0, 0)),
            fixed_spec((1, 1, rows, depth * width), (which, half, 0, 0)),
        ]
        + [raw_spec] * last,
        out_specs=whole_spec(result) if last else raw_spec,
        scratch_shapes=[pltpu.VMEM((rows, length), F32)] * last,
        compiler_params=params(16),
        cost_estimate=cost(2 * rows * 3 * length * depth * width, 1e7),
        name="weight_gradient",
    )(*([field, errors] + [before] * last))


def unpack_kernel(packed, *outs):
    channels = packed.shape[0]
    fit = 128 // channels
    for k, out in enumerate(outs):
        for a in range(3):
            for t in range(9):
                at = 8 * a + t if t < 8 else 24 + a
                at += 32 * k
                lane = at % fit * channels
                out[9 * a + t] = packed[:, at // fit, lane : lane + channels]


def unpack(packed):
    channels = packed.shape[0]
    shape = (27, channels, channels)
    return pl.pallas_call(
        unpack_kernel,
        out_shape=[jax.ShapeDtypeStruct(shape, F32)] * 2,
        grid=(1,),
        in_specs=[whole_spec(packed.shape)],
        out_specs=[whole_spec(shape)] * 2,
        compiler_params=params(16),
        name="unpack",
    )(packed)


def total_over_devices(value, scale):
    axes = ("depth", "group")
    devices = lax.axis_size("depth") * lax.axis_size("group")
    shares = lax.all_to_all(value.reshape(devices, -1, 128), axes, 0, 0)
    share = jnp.sum(shares, axis=0) * scale
    everyone = lax.all_to_all(jnp.broadcast_to(share[None], shares.shape), axes, 0, 0)
    return everyone


def shift_along(value, axis, step):
    size = lax.axis_size(axis)
    return lax.ppermute(value, axis, [(i + step, i) for i in range(size) if 0 <= i + step < size])


def exchange_sides(faces):
    zlo, zhi, ylo, yhi = faces
    return shift_along(yhi, "group", -1), shift_along(ylo, "group", 1)


def exchange_faces(faces, sides, width):
    zlo, zhi, _, _ = faces
    low, high = sides
    first = jnp.concatenate([zlo, low[:, :, :width], high[:, :, :width]], axis=1)
    last = jnp.concatenate([zhi, low[:, :, -width:], high[:, :, -width:]], axis=1)
    return [shift_along(last, "depth", -1), shift_along(first, "depth", 1), low, high]


def after(value, others):
    return lax.optimization_barrier((value, others))[0]


def local(
    output_one, output_two, cotangent_one, cotangent_two, first_weight, second_weight, bricks
):
    brick_edge = output_one.shape[1]
    width = output_one.shape[3]
    slots = bricks.shape[2]
    groups = lax.axis_size("group")
    position = lax.axis_index("group")
    own_list = bricks[0][position]
    present = jnp.any(own_list[:, None] == jnp.arange(slots, dtype=jnp.int32)[None, :], axis=0)
    mask = jnp.repeat(present.astype(F32), brick_edge)[None, :]

    upper, *faces = upper_parts(output_one, mask)
    sides = exchange_sides(faces)

    def turned(kernel):
        return jnp.transpose(jnp.flip(kernel, 0), (0, 2, 1))

    taps_g = banded(jnp.stack([second_weight, turned(second_weight)]))
    sides = after(sides, taps_g)
    upper_halos = exchange_faces(faces, sides, width)
    taps_f = banded(jnp.stack([first_weight, turned(first_weight)]))
    upper = after(upper, taps_f)

    restored_two, middle, *faces, field = conv_call(
        first_kernel, mask, [(taps_g, 0)], upper, upper_halos, [output_two, cotangent_two], 1, 2, 1, "first_conv"
    )
    sides = exchange_sides(faces)
    second_a = weight_gradient(field, middle, 1, 0, width)
    sides = after(sides, second_a)
    middle_halos = exchange_faces(faces, sides, width)
    second_total = weight_gradient(field, middle, 1, 1, width, second_a)
    restored_one, input_grad_one, last, *faces, field = conv_call(
        second_kernel,
        mask,
        [(taps_f, 0), (taps_g, 1)],
        middle,
        middle_halos,
        [output_one, cotangent_one],
        2,
        1,
        2,
        "second_conv",
    )
    sides = exchange_sides(faces)
    first_a = weight_gradient(field, last, 0, 0, width)
    sides = after(sides, first_a)
    last_halos = exchange_faces(faces, sides, width)
    first_total = weight_gradient(field, last, 0, 1, width, first_a)
    (input_grad_two,) = conv_call(
        third_kernel, mask, [(taps_f, 1)], last, last_halos, [cotangent_two], 1, 0, 1, "third_conv"
    )
    scale = 1.0 / math.sqrt(
        float(brick_edge * lax.axis_size("depth") * output_one.shape[2] * groups * width)
    )
    packed = jnp.concatenate([first_total, second_total], axis=1)
    first_total, second_total = unpack(total_over_devices(packed, scale).reshape(packed.shape[0], -1, 128))
    return (restored_one, restored_two, input_grad_one, input_grad_two, first_total, second_total)


def solution(mesh):
    slab = P(None, "depth", "group", None)
    return jax.shard_map(
        local,
        mesh=mesh,
        in_specs=(slab, slab, slab, slab, P(), P(), P("depth", None, None)),
        out_specs=(slab, slab, slab, slab, P(), P()),
        check_vma=False,
    )
```

```python
import functools
import math

import jax
import jax.numpy as jnp
from jax import lax
from jax.experimental import pallas as pl
from jax.experimental.pallas import tpu as pltpu
from jax.sharding import PartitionSpec as P

BF = jnp.bfloat16
F32 = jnp.float32
HALF = 8


def shifted(plane, step):
    if step == 0:
        return plane
    width = plane.shape[1]
    lane = lax.broadcasted_iota(jnp.int32, plane.shape, 1)
    edge = 0 if step < 0 else width - 1
    rolled = pltpu.roll(plane, (-step) % width, axis=1)
    return jnp.where(lane == edge, jnp.zeros_like(rolled), rolled)


def picker(rows):
    channels = rows // HALF
    out = lax.broadcasted_iota(jnp.int32, (2 * channels, rows), 0)
    col = lax.broadcasted_iota(jnp.int32, (2 * channels, rows), 1)
    wanted = (out % channels) * HALF + jnp.where(out < channels, 0, HALF - 1)
    return jnp.where(col == wanted, 1.0, 0.0).astype(BF)


def build_field(field, f, centre, halos, width):
    zlo, zhi, ylo, yhi = halos
    rows = centre.shape[2]
    channels = rows // HALF
    depth = centre.shape[3] // width
    pick = picker(rows)
    side = 2 * channels
    plain = ((0, rows), (3 * rows, side))

    def unshifted(lanes, mains, low, high):
        for half in range(2):
            ends = jnp.dot(pick, mains[1 - half], preferred_element_type=F32).astype(BF)
            sides = [low, ends[:channels]] if half == 0 else [ends[channels:], high]
            field[half, rows : 2 * rows, lanes] = mains[half]
            field[half, 3 * rows + side : 3 * rows + 2 * side, lanes] = jnp.concatenate(sides, axis=0)

    for start, face in ((0, zlo), ((depth + 1) * width, zhi)):
        unshifted(
            slice(start, start + width),
            [face[f, 0:rows, :], face[f, rows : 2 * rows, :]],
            face[f, 2 * rows : 2 * rows + channels, :],
            face[f, 2 * rows + channels :, :],
        )
    unshifted(slice(width, (depth + 1) * width), [centre[f, 0], centre[f, 1]], ylo[f], yhi[f])

    def plane(number, carry):
        lanes = pl.ds(pl.multiple_of(number * width, width), width)
        for half in range(2):
            for start, size in plain:
                block = field[half, start + size : start + 2 * size, lanes]
                field[half, start : start + size, lanes] = shifted(block, -1)
                field[half, start + 2 * size : start + 3 * size, lanes] = shifted(block, 1)
        return carry

    lax.fori_loop(0, depth + 2, plane, 0, unroll=6)


def convolve(field, half, taps, pair, width):
    total = None
    for step in range(3):
        lanes = pl.ds(pl.multiple_of((2 * pair + step) * width, width), 2 * width)
        term = jnp.dot(taps[step], field[half, :, lanes], preferred_element_type=F32)
        total = term if total is None else total + term
    return total


def to_native(first, second, part, width):
    lanes = slice(part * width, (part + 1) * width)
    channels = first.shape[0] // HALF
    return jnp.concatenate(
        [first[:, lanes].reshape(channels, HALF, width), second[:, lanes].reshape(channels, HALF, width)], axis=1
    )


def write_parts(f, pair, planes, outs, depth):
    centre, zlo, zhi, ylo, yhi = outs
    channels, tall, width = planes[0].shape
    rows = channels * HALF
    lanes = pl.ds(pl.multiple_of(pair * 2 * width, width), 2 * width)
    pick = picker(rows)
    halves = []
    for half in range(2):
        block = jnp.concatenate(
            [p[:, half * HALF : (half + 1) * HALF, :].reshape(rows, width) for p in planes], axis=1
        ).astype(BF)
        centre[f, half] = block
        halves.append(block)
    low = jnp.dot(pick, halves[0], preferred_element_type=F32).astype(BF)[:channels]
    high = jnp.dot(pick, halves[1], preferred_element_type=F32).astype(BF)[channels:]
    ylo[f, :, lanes] = low
    yhi[f, :, lanes] = high

    @pl.when(pair == 0)
    def _():
        for half in range(2):
            zlo[f, half * rows : (half + 1) * rows, :] = halves[half][:, :width]

    @pl.when(pair == depth // 2 - 1)
    def _():
        for half in range(2):
            zhi[f, half * rows : (half + 1) * rows, :] = halves[half][:, width:]


def part_shapes(fields, channels, depth, width):
    rows = channels * HALF
    face = (fields, 2 * rows, width)
    side = (fields, channels, depth * width)
    return [(fields, 2, rows, depth * width), face, face, side, side]


def whole_spec(shape):
    return pl.BlockSpec(shape, lambda i: (0,) * len(shape))


def part_specs(shapes, width):
    fields, halves, rows, _ = shapes[0]
    centre = pl.BlockSpec((fields, halves, rows, 2 * width), lambda i: (0, 0, 0, i))
    return [centre] + [whole_spec(s) for s in shapes[1:]]


def fixed_spec(shape, index=None):
    index = index or (0,) * len(shape)
    return pl.BlockSpec(shape, lambda i: index, pipeline_mode=pl.Buffered(1))


def pair_spec(shape):
    channels, _, tall, width = shape
    return pl.BlockSpec((channels, 2, tall, width), lambda i: (0, i, 0, 0))


def params(mebibytes):
    return pltpu.CompilerParams(dimension_semantics=("arbitrary",), vmem_limit_bytes=mebibytes * 1024 * 1024)


def streamed(value):
    return pltpu.with_memory_space_constraint(value, pltpu.HBM)


def cost(flops, nbytes):
    return pl.CostEstimate(flops=int(flops), bytes_accessed=int(nbytes), transcendentals=0)


def upper_kernel(depth, source, mask, *outs):
    pair = pl.program_id(0)
    m = mask[...][None]
    planes = [source[:, part].astype(F32) * m for part in range(2)]
    write_parts(0, pair, planes, outs, depth)


def upper_parts(source, mask):
    channels, depth, tall, width = source.shape
    shapes = part_shapes(1, channels, depth, width)
    return pl.pallas_call(
        functools.partial(upper_kernel, depth),
        out_shape=[pltpu.HBM(shapes[0], BF)] + [jax.ShapeDtypeStruct(s, BF) for s in shapes[1:]],
        grid=(depth // 2,),
        in_specs=[pair_spec(source.shape), whole_spec(mask.shape)],
        out_specs=part_specs(shapes, width),
        compiler_params=params(16),
        cost_estimate=cost(1e8, 6e6),
        name="upper_parts",
    )(source, mask)


def taps_kernel(taps, out):
    channels = taps.shape[3]
    rows = channels * HALF
    chan = lax.broadcasted_iota(jnp.int32, (channels, rows), 0)
    col = lax.broadcasted_iota(jnp.int32, (channels, rows), 1)
    spread = jnp.where(col // HALF == chan, 1.0, 0.0).astype(BF)
    row_at = lax.broadcasted_iota(jnp.int32, (channels, HALF, rows), 1)
    col_at = lax.broadcasted_iota(jnp.int32, (channels, HALF, rows), 2) % HALF
    gap = col_at - row_at
    width = 6 * channels
    place_row = lax.broadcasted_iota(jnp.int32, (channels, width), 0)
    place_col = lax.broadcasted_iota(jnp.int32, (channels, width), 1)
    side_row = lax.broadcasted_iota(jnp.int32, (channels, HALF, width), 1)
    side_lane = lax.broadcasted_iota(jnp.int32, (channels, HALF, width), 2) // channels % 2
    keep = ((side_row == 0) & (side_lane == 0)) | ((side_row == HALF - 1) & (side_lane == 1))
    for a in range(3):
        for c in range(3):
            wide = [
                jnp.dot(taps[0, 9 * a + 3 * b + c], spread, preferred_element_type=F32)[:, None, :] for b in range(3)
            ]
            block = jnp.where(gap == 0, wide[1], 0.0)
            block = jnp.where(gap == -1, wide[0], block)
            block = jnp.where(gap == 1, wide[2], block)
            out[0, a, :, c * rows : (c + 1) * rows] = block.reshape(rows, rows).astype(BF)
        edge = None
        for c in range(3):
            for end in range(2):
                place = jnp.where(place_col == (2 * c + end) * channels + place_row, 1.0, 0.0).astype(BF)
                term = jnp.dot(taps[0, 9 * a + 6 * end + c], place, preferred_element_type=F32)
                edge = term if edge is None else edge + term
        edge = jnp.where(keep, edge[:, None, :], 0.0)
        out[0, a, :, 3 * rows :] = edge.reshape(rows, width).astype(BF)


def banded(kernels):
    count, taps, channels, _ = kernels.shape
    rows = channels * HALF
    length = 3 * rows + 6 * channels
    return pl.pallas_call(
        taps_kernel,
        out_shape=pltpu.HBM((count, 3, rows, length), BF),
        grid=(count,),
        in_specs=[
            pl.BlockSpec((1, taps, channels, channels), lambda i: (i, 0, 0, 0)),
        ],
        out_specs=pl.BlockSpec((1, 3, rows, length), lambda i: (i, 0, 0, 0)),
        compiler_params=params(16),
        cost_estimate=cost(1e9, 8e6),
        name="banded_taps",
    )(kernels)


def first_kernel(depth, width, mask, taps, centre, *refs):
    halos, (output_two, cotangent_two), restored, parts, field = refs[:4], refs[4:6], refs[6], refs[7:12], refs[13]
    pair = pl.program_id(0)
    kept = pltpu.make_async_copy(field, refs[12], refs[14])

    @pl.when(pair == 0)
    def _():
        build_field(field, 0, centre, halos, width)
        kept.start()

    m = mask[...][None]
    sums = [convolve(field, half, taps.at[0], pair, width) for half in range(2)]
    lower, errors = [], []
    for part in range(2):
        preact = to_native(sums[0], sums[1], part, width)
        s = jax.nn.sigmoid(preact)
        inside = m * s
        silu = preact * inside
        shaped = silu.astype(BF).astype(F32)
        slope = inside + silu * (1.0 - s)
        out = (output_two[:, part].astype(F32) - shaped).astype(BF)
        restored[:, part] = out
        lower.append(out.astype(F32) * m)
        errors.append(cotangent_two[:, part].astype(F32) * slope)
    write_parts(0, pair, lower, parts, depth)
    write_parts(1, pair, errors, parts, depth)

    @pl.when(pair == depth // 2 - 1)
    def _():
        kept.wait()


def second_kernel(depth, width, mask, taps_f, taps_g, centre, *refs):
    halos, (output_one, cotangent_one) = refs[:4], refs[4:6]
    restored, grad, parts = refs[6], refs[7], refs[8:13]
    field_l, field_e = refs[14], refs[15]
    kept = pltpu.make_async_copy(field_l, refs[13], refs[16])
    pair = pl.program_id(0)

    @pl.when(pair == 0)
    def _():
        build_field(field_l, 0, centre, halos, width)
        kept.start()
        build_field(field_e, 1, centre, halos, width)

    m = mask[...][None]
    sums = [convolve(field_l, half, taps_f.at[0], pair, width) for half in range(2)]
    spreads = [convolve(field_e, half, taps_g.at[0], pair, width) for half in range(2)]
    errors = []
    for part in range(2):
        preact = to_native(sums[0], sums[1], part, width)
        spread = to_native(spreads[0], spreads[1], part, width)
        s = jax.nn.sigmoid(preact)
        inside = m * s
        silu = preact * inside
        shaped = silu.astype(BF).astype(F32)
        slope = inside + silu * (1.0 - s)
        restored[:, part] = (output_one[:, part].astype(F32) - shaped).astype(BF)
        total = (cotangent_one[:, part].astype(F32) + m * spread).astype(BF)
        grad[:, part] = total
        errors.append(total.astype(F32) * slope)
    write_parts(0, pair, errors, parts, depth)

    @pl.when(pair == depth // 2 - 1)
    def _():
        kept.wait()


def third_kernel(depth, width, mask, taps, centre, *refs):
    halos, cotangent_two, grad, field = refs[:4], refs[4], refs[5], refs[6]
    pair = pl.program_id(0)

    @pl.when(pair == 0)
    def _():
        build_field(field, 0, centre, halos, width)

    m = mask[...][None]
    sums = [convolve(field, half, taps.at[0], pair, width) for half in range(2)]
    for part in range(2):
        spread = to_native(sums[0], sums[1], part, width)
        grad[:, part] = (cotangent_two[:, part].astype(F32) + m * spread).astype(BF)


def conv_call(kernel, mask, matrices, centre, halos, natives, n_native_out, out_fields, fields, name):
    channels, depth, tall, width = natives[0].shape
    rows = channels * HALF
    length = matrices[0][0].shape[3]
    shapes = part_shapes(out_fields, channels, depth, width) if out_fields else []
    tap_specs = [
        fixed_spec((1, 3, rows, length), (k, 0, 0, 0)) for _, k in matrices
    ]
    native = natives[0].shape
    held = (2, length, (depth + 2) * width)
    export = 1 if out_fields else 0
    return pl.pallas_call(
        functools.partial(kernel, depth, width),
        out_shape=[jax.ShapeDtypeStruct(native, BF)] * n_native_out + [jax.ShapeDtypeStruct(s, BF) for s in shapes]
        + [jax.ShapeDtypeStruct(held, BF)] * export,
        grid=(depth // 2,),
        in_specs=[fixed_spec(mask.shape)]
        + tap_specs
        + [fixed_spec(centre.shape)]
        + [fixed_spec(h.shape) for h in halos]
        + [pair_spec(native)] * len(natives),
        out_specs=[pair_spec(native)] * n_native_out
        + (part_specs(shapes, width) if shapes else [])
        + [pl.BlockSpec(memory_space=pl.ANY)] * export,
        scratch_shapes=[pltpu.VMEM(held, BF)] * fields + [pltpu.SemaphoreType.DMA] * export,
        compiler_params=params(22 + 12 * (fields - 1)),
        cost_estimate=cost(2 * 2 * rows * 3 * length * depth * width * fields, 2e7),
        name=name,
    )(mask, *[streamed(m) for m, _ in matrices], centre, *halos, *[streamed(v) for v in natives])


def gradient_half_kernel(depth, width, field, errors, out):
    lanes = pl.ds(pl.multiple_of(pl.program_id(0) * width, width), depth * width)
    out[0] = lax.dot_general(
        errors[0, 0], field[0, :, lanes], (((1,), (1,)), ((), ())), preferred_element_type=F32
    )


def gradient_kernel(depth, width, field, errors, before, out, products):
    rows = errors.shape[2]
    channels = rows // HALF
    a = pl.program_id(0)
    lanes = pl.ds(pl.multiple_of(a * width, width), depth * width)

    products[...] = before[0] + lax.dot_general(
        errors[0, 0], field[0, :, lanes], (((1,), (1,)), ((), ())), preferred_element_type=F32
    )

    def pieces(value):
        high = value.astype(BF)
        return high, (value - high.astype(F32)).astype(BF)

    def tile(size):
        row = lax.broadcasted_iota(jnp.int32, (2 * HALF, size), 0) % HALF
        return row, lax.broadcasted_iota(jnp.int32, (2 * HALF, size), 1)

    gather_row = lax.broadcasted_iota(jnp.int32, (channels, rows), 0)
    gather_col = lax.broadcasted_iota(jnp.int32, (channels, rows), 1)
    gather = jnp.where(gather_col // HALF == gather_row, 1.0, 0.0).astype(BF)

    def chosen(parts, keep):
        total = None
        for part in parts:
            size = part.shape[1]
            kept = (part.reshape(rows // (2 * HALF), 2 * HALF, size) * keep[None]).reshape(rows, size)
            term = jnp.dot(gather, kept, preferred_element_type=F32)
            total = term if total is None else total + term
        return total

    row, col = tile(rows)
    bands = [jnp.where(col % HALF - row == b - 1, 1.0, 0.0).astype(BF) for b in range(3)]
    picked = {}
    for c in range(3):
        parts = pieces(products[:, c * rows : (c + 1) * rows])
        for b in range(3):
            picked[b, c] = chosen(parts, bands[b])
    row, col = tile(6 * channels)
    ends = jnp.where(row == jnp.where(col // channels % 2 == 0, 0, HALF - 1), 1.0, 0.0).astype(BF)
    sides = chosen(pieces(products[:, 3 * rows :]), ends)
    fold_row = lax.broadcasted_iota(jnp.int32, (rows, channels), 0)
    fold_col = lax.broadcasted_iota(jnp.int32, (rows, channels), 1)
    fold = jnp.where(fold_row // HALF == fold_col, 1.0, 0.0).astype(BF)
    summed = None
    for piece in pieces(jnp.concatenate([picked[b, c] for b in range(3) for c in range(3)], axis=0)):
        term = jnp.dot(piece, fold, preferred_element_type=F32)
        summed = term if summed is None else summed + term
    values = []
    for b in range(3):
        for c in range(3):
            at = (3 * b + c) * channels
            value = summed[at : at + channels]
            if b != 1:
                at = (2 * c + b // 2) * channels
                value = value + sides[:, at : at + channels]
            values.append(value)
    out[:, pl.ds(pl.multiple_of(a * 8 * channels, 8 * channels), 8 * channels)] = jnp.concatenate(values[:8], axis=1)
    empty = jnp.zeros((channels, channels), F32)
    tail = jnp.concatenate([jnp.where(a == k, values[8], empty) for k in range(3)] + [empty] * 5, axis=1)
    last = slice(24 * channels, 32 * channels)

    @pl.when(a == 0)
    def _():
        out[:, last] = tail

    @pl.when(a > 0)
    def _():
        out[:, last] = out[:, last] + tail


def weight_gradient(field, errors, which, half, width, before=None):
    _, length, columns = field.shape
    rows = errors.shape[2]
    channels = rows // HALF
    depth = errors.shape[3] // width
    raw = (3, rows, length)
    raw_spec = pl.BlockSpec((1, rows, length), lambda i: (i, 0, 0))
    last = before is not None
    result = (channels, 32 * channels) if last else raw
    return pl.pallas_call(
        functools.partial(gradient_kernel if last else gradient_half_kernel, depth, width),
        out_shape=jax.ShapeDtypeStruct(result, F32),
        grid=(3,),
        in_specs=[
            fixed_spec((1, length, columns), (half, 0, 0)),
            fixed_spec((1, 1, rows, depth * width), (which, half, 0, 0)),
        ]
        + [raw_spec] * last,
        out_specs=whole_spec(result) if last else raw_spec,
        scratch_shapes=[pltpu.VMEM((rows, length), F32)] * last,
        compiler_params=params(16),
        cost_estimate=cost(2 * rows * 3 * length * depth * width, 1e7),
        name="weight_gradient",
    )(*([field, errors] + [before] * last))


def unpack_kernel(packed, *outs):
    channels = packed.shape[0]
    fit = 128 // channels
    for k, out in enumerate(outs):
        for a in range(3):
            for t in range(9):
                at = 8 * a + t if t < 8 else 24 + a
                at += 32 * k
                lane = at % fit * channels
                out[9 * a + t] = packed[:, at // fit, lane : lane + channels]


def unpack(packed):
    channels = packed.shape[0]
    shape = (27, channels, channels)
    return pl.pallas_call(
        unpack_kernel,
        out_shape=[jax.ShapeDtypeStruct(shape, F32)] * 2,
        grid=(1,),
        in_specs=[whole_spec(packed.shape)],
        out_specs=[whole_spec(shape)] * 2,
        compiler_params=params(16),
        name="unpack",
    )(packed)


def total_over_devices(value, scale):
    axes = ("depth", "group")
    devices = lax.axis_size("depth") * lax.axis_size("group")
    shares = lax.all_to_all(value.reshape(devices, -1, 128), axes, 0, 0)
    share = jnp.sum(shares, axis=0) * scale
    everyone = lax.all_to_all(jnp.broadcast_to(share[None], shares.shape), axes, 0, 0)
    return everyone


def shift_along(value, axis, step):
    size = lax.axis_size(axis)
    return lax.ppermute(value, axis, [(i + step, i) for i in range(size) if 0 <= i + step < size])


def exchange_sides(faces):
    zlo, zhi, ylo, yhi = faces
    return shift_along(yhi, "group", -1), shift_along(ylo, "group", 1)


def exchange_faces(faces, sides, width):
    zlo, zhi, _, _ = faces
    low, high = sides
    first = jnp.concatenate([zlo, low[:, :, :width], high[:, :, :width]], axis=1)
    last = jnp.concatenate([zhi, low[:, :, -width:], high[:, :, -width:]], axis=1)
    return [shift_along(last, "depth", -1), shift_along(first, "depth", 1), low, high]


def after(value, others):
    return lax.optimization_barrier((value, others))[0]


def local(
    output_one, output_two, cotangent_one, cotangent_two, first_weight, second_weight, bricks
):
    brick_edge = output_one.shape[1]
    width = output_one.shape[3]
    slots = bricks.shape[2]
    groups = lax.axis_size("group")
    position = lax.axis_index("group")
    own_list = bricks[0][position]
    present = jnp.any(own_list[:, None] == jnp.arange(slots, dtype=jnp.int32)[None, :], axis=0)
    mask = jnp.repeat(present.astype(F32), brick_edge)[None, :]

    upper, *faces = upper_parts(output_one, mask)
    sides = exchange_sides(faces)

    def turned(kernel):
        return jnp.transpose(jnp.flip(kernel, 0), (0, 2, 1))

    taps_g = banded(jnp.stack([second_weight, turned(second_weight)]))
    sides = after(sides, taps_g)
    upper_halos = exchange_faces(faces, sides, width)
    taps_f = banded(jnp.stack([first_weight, turned(first_weight)]))
    upper = after(upper, taps_f)

    restored_two, middle, *faces, field = conv_call(
        first_kernel, mask, [(taps_g, 0)], upper, upper_halos, [output_two, cotangent_two], 1, 2, 1, "first_conv"
    )
    sides = exchange_sides(faces)
    second_a = weight_gradient(field, middle, 1, 0, width)
    sides = after(sides, second_a)
    middle_halos = exchange_faces(faces, sides, width)
    second_total = weight_gradient(field, middle, 1, 1, width, second_a)
    restored_one, input_grad_one, last, *faces, field = conv_call(
        second_kernel,
        mask,
        [(taps_f, 0), (taps_g, 1)],
        middle,
        middle_halos,
        [output_one, cotangent_one],
        2,
        1,
        2,
        "second_conv",
    )
    sides = exchange_sides(faces)
    first_a = weight_gradient(field, last, 0, 0, width)
    sides = after(sides, first_a)
    last_halos = exchange_faces(faces, sides, width)
    first_total = weight_gradient(field, last, 0, 1, width, first_a)
    (input_grad_two,) = conv_call(
        third_kernel, mask, [(taps_f, 1)], last, last_halos, [cotangent_two], 1, 0, 1, "third_conv"
    )
    scale = 1.0 / math.sqrt(
        float(brick_edge * lax.axis_size("depth") * output_one.shape[2] * groups * width)
    )
    packed = jnp.concatenate([first_total, second_total], axis=1)
    first_total, second_total = unpack(total_over_devices(packed, scale).reshape(packed.shape[0], -1, 128))
    return (restored_one, restored_two, input_grad_one, input_grad_two, first_total, second_total)


def solution(mesh):
    slab = P(None, "depth", "group", None)
    return jax.shard_map(
        local,
        mesh=mesh,
        in_specs=(slab, slab, slab, slab, P(), P(), P("depth", None, None)),
        out_specs=(slab, slab, slab, slab, P(), P()),
        check_vma=False,
    )
```

```python
import functools
import math

import jax
import jax.numpy as jnp
from jax import lax
from jax.experimental import pallas as pl
from jax.experimental.pallas import tpu as pltpu
from jax.sharding import PartitionSpec as P

BF = jnp.bfloat16
F32 = jnp.float32
HALF = 8


def shifted(plane, step):
    if step == 0:
        return plane
    width = plane.shape[1]
    lane = lax.broadcasted_iota(jnp.int32, plane.shape, 1)
    edge = 0 if step < 0 else width - 1
    rolled = pltpu.roll(plane, (-step) % width, axis=1)
    return jnp.where(lane == edge, jnp.zeros_like(rolled), rolled)


def picker(rows):
    channels = rows // HALF
    out = lax.broadcasted_iota(jnp.int32, (2 * channels, rows), 0)
    col = lax.broadcasted_iota(jnp.int32, (2 * channels, rows), 1)
    wanted = (out % channels) * HALF + jnp.where(out < channels, 0, HALF - 1)
    return jnp.where(col == wanted, 1.0, 0.0).astype(BF)


def build_field(field, f, centre, halos, width):
    zlo, zhi, ylo, yhi = halos
    rows = centre.shape[2]
    channels = rows // HALF
    depth = centre.shape[3] // width
    pick = picker(rows)
    side = 2 * channels
    plain = ((0, rows), (3 * rows, side))

    def unshifted(lanes, mains, low, high):
        for half in range(2):
            ends = jnp.dot(pick, mains[1 - half], preferred_element_type=F32).astype(BF)
            sides = [low, ends[:channels]] if half == 0 else [ends[channels:], high]
            field[half, rows : 2 * rows, lanes] = mains[half]
            field[half, 3 * rows + side : 3 * rows + 2 * side, lanes] = jnp.concatenate(sides, axis=0)

    for start, face in ((0, zlo), ((depth + 1) * width, zhi)):
        unshifted(
            slice(start, start + width),
            [face[f, 0:rows, :], face[f, rows : 2 * rows, :]],
            face[f, 2 * rows : 2 * rows + channels, :],
            face[f, 2 * rows + channels :, :],
        )
    unshifted(slice(width, (depth + 1) * width), [centre[f, 0], centre[f, 1]], ylo[f], yhi[f])

    def plane(number, carry):
        lanes = pl.ds(pl.multiple_of(number * width, width), width)
        for half in range(2):
            for start, size in plain:
                block = field[half, start + size : start + 2 * size, lanes]
                field[half, start : start + size, lanes] = shifted(block, -1)
                field[half, start + 2 * size : start + 3 * size, lanes] = shifted(block, 1)
        return carry

    lax.fori_loop(0, depth + 2, plane, 0, unroll=6)


def convolve(field, half, taps, pair, width):
    total = None
    for step in range(3):
        lanes = pl.ds(pl.multiple_of((2 * pair + step) * width, width), 2 * width)
        term = jnp.dot(taps[step], field[half, :, lanes], preferred_element_type=F32)
        total = term if total is None else total + term
    return total


def to_native(first, second, part, width):
    lanes = slice(part * width, (part + 1) * width)
    channels = first.shape[0] // HALF
    return jnp.concatenate(
        [first[:, lanes].reshape(channels, HALF, width), second[:, lanes].reshape(channels, HALF, width)], axis=1
    )


def write_parts(f, pair, planes, outs, depth):
    centre, zlo, zhi, ylo, yhi = outs
    channels, tall, width = planes[0].shape
    rows = channels * HALF
    lanes = pl.ds(pl.multiple_of(pair * 2 * width, width), 2 * width)
    pick = picker(rows)
    halves = []
    for half in range(2):
        block = jnp.concatenate(
            [p[:, half * HALF : (half + 1) * HALF, :].reshape(rows, width) for p in planes], axis=1
        ).astype(BF)
        centre[f, half] = block
        halves.append(block)
    low = jnp.dot(pick, halves[0], preferred_element_type=F32).astype(BF)[:channels]
    high = jnp.dot(pick, halves[1], preferred_element_type=F32).astype(BF)[channels:]
    ylo[f, :, lanes] = low
    yhi[f, :, lanes] = high

    @pl.when(pair == 0)
    def _():
        for half in range(2):
            zlo[f, half * rows : (half + 1) * rows, :] = halves[half][:, :width]

    @pl.when(pair == depth // 2 - 1)
    def _():
        for half in range(2):
            zhi[f, half * rows : (half + 1) * rows, :] = halves[half][:, width:]


def part_shapes(fields, channels, depth, width):
    rows = channels * HALF
    face = (fields, 2 * rows, width)
    side = (fields, channels, depth * width)
    return [(fields, 2, rows, depth * width), face, face, side, side]


def whole_spec(shape):
    return pl.BlockSpec(shape, lambda i: (0,) * len(shape))


def part_specs(shapes, width):
    fields, halves, rows, _ = shapes[0]
    centre = pl.BlockSpec((fields, halves, rows, 2 * width), lambda i: (0, 0, 0, i))
    return [centre] + [whole_spec(s) for s in shapes[1:]]


def fixed_spec(shape, index=None):
    index = index or (0,) * len(shape)
    return pl.BlockSpec(shape, lambda i: index, pipeline_mode=pl.Buffered(1))


def pair_spec(shape):
    channels, _, tall, width = shape
    return pl.BlockSpec((channels, 2, tall, width), lambda i: (0, i, 0, 0))


def params(mebibytes):
    return pltpu.CompilerParams(dimension_semantics=("arbitrary",), vmem_limit_bytes=mebibytes * 1024 * 1024)


def streamed(value):
    return pltpu.with_memory_space_constraint(value, pltpu.HBM)


def cost(flops, nbytes):
    return pl.CostEstimate(flops=int(flops), bytes_accessed=int(nbytes), transcendentals=0)


def upper_kernel(depth, source, mask, *outs):
    pair = pl.program_id(0)
    m = mask[...][None]
    planes = [source[:, part].astype(F32) * m for part in range(2)]
    write_parts(0, pair, planes, outs, depth)


def upper_parts(source, mask):
    channels, depth, tall, width = source.shape
    shapes = part_shapes(1, channels, depth, width)
    return pl.pallas_call(
        functools.partial(upper_kernel, depth),
        out_shape=[jax.ShapeDtypeStruct(s, BF) for s in shapes],
        grid=(depth // 2,),
        in_specs=[pair_spec(source.shape), whole_spec(mask.shape)],
        out_specs=part_specs(shapes, width),
        compiler_params=params(16),
        cost_estimate=cost(1e8, 6e6),
        name="upper_parts",
    )(source, mask)


def taps_kernel(taps, out):
    channels = taps.shape[3]
    rows = channels * HALF
    chan = lax.broadcasted_iota(jnp.int32, (channels, rows), 0)
    col = lax.broadcasted_iota(jnp.int32, (channels, rows), 1)
    spread = jnp.where(col // HALF == chan, 1.0, 0.0).astype(BF)
    row_at = lax.broadcasted_iota(jnp.int32, (channels, HALF, rows), 1)
    col_at = lax.broadcasted_iota(jnp.int32, (channels, HALF, rows), 2) % HALF
    gap = col_at - row_at
    width = 6 * channels
    place_row = lax.broadcasted_iota(jnp.int32, (channels, width), 0)
    place_col = lax.broadcasted_iota(jnp.int32, (channels, width), 1)
    side_row = lax.broadcasted_iota(jnp.int32, (channels, HALF, width), 1)
    side_lane = lax.broadcasted_iota(jnp.int32, (channels, HALF, width), 2) // channels % 2
    keep = ((side_row == 0) & (side_lane == 0)) | ((side_row == HALF - 1) & (side_lane == 1))
    for a in range(3):
        for c in range(3):
            wide = [
                jnp.dot(taps[0, 9 * a + 3 * b + c], spread, preferred_element_type=F32)[:, None, :] for b in range(3)
            ]
            block = jnp.where(gap == 0, wide[1], 0.0)
            block = jnp.where(gap == -1, wide[0], block)
            block = jnp.where(gap == 1, wide[2], block)
            out[0, a, :, c * rows : (c + 1) * rows] = block.reshape(rows, rows).astype(BF)
        edge = None
        for c in range(3):
            for end in range(2):
                place = jnp.where(place_col == (2 * c + end) * channels + place_row, 1.0, 0.0).astype(BF)
                term = jnp.dot(taps[0, 9 * a + 6 * end + c], place, preferred_element_type=F32)
                edge = term if edge is None else edge + term
        edge = jnp.where(keep, edge[:, None, :], 0.0)
        out[0, a, :, 3 * rows :] = edge.reshape(rows, width).astype(BF)


def banded(kernels):
    count, taps, channels, _ = kernels.shape
    rows = channels * HALF
    length = 3 * rows + 6 * channels
    return pl.pallas_call(
        taps_kernel,
        out_shape=pltpu.HBM((count, 3, rows, length), BF),
        grid=(count,),
        in_specs=[
            pl.BlockSpec((1, taps, channels, channels), lambda i: (i, 0, 0, 0)),
        ],
        out_specs=pl.BlockSpec((1, 3, rows, length), lambda i: (i, 0, 0, 0)),
        compiler_params=params(16),
        cost_estimate=cost(1e9, 8e6),
        name="banded_taps",
    )(kernels)


def first_kernel(depth, width, mask, taps, centre, *refs):
    halos, (output_two, cotangent_two), restored, parts, field = refs[:4], refs[4:6], refs[6], refs[7:12], refs[13]
    pair = pl.program_id(0)
    kept = pltpu.make_async_copy(field, refs[12], refs[14])

    @pl.when(pair == 0)
    def _():
        build_field(field, 0, centre, halos, width)
        kept.start()

    m = mask[...][None]
    sums = [convolve(field, half, taps.at[0], pair, width) for half in range(2)]
    lower, errors = [], []
    for part in range(2):
        preact = to_native(sums[0], sums[1], part, width)
        s = jax.nn.sigmoid(preact)
        inside = m * s
        silu = preact * inside
        shaped = silu.astype(BF).astype(F32)
        slope = inside + silu * (1.0 - s)
        out = (output_two[:, part].astype(F32) - shaped).astype(BF)
        restored[:, part] = out
        lower.append(out.astype(F32) * m)
        errors.append(cotangent_two[:, part].astype(F32) * slope)
    write_parts(0, pair, lower, parts, depth)
    write_parts(1, pair, errors, parts, depth)

    @pl.when(pair == depth // 2 - 1)
    def _():
        kept.wait()


def second_kernel(depth, width, mask, taps_f, taps_g, centre, *refs):
    halos, (output_one, cotangent_one) = refs[:4], refs[4:6]
    restored, grad, parts = refs[6], refs[7], refs[8:13]
    field_l, field_e = refs[14], refs[15]
    kept = pltpu.make_async_copy(field_l, refs[13], refs[16])
    pair = pl.program_id(0)

    @pl.when(pair == 0)
    def _():
        build_field(field_l, 0, centre, halos, width)
        kept.start()
        build_field(field_e, 1, centre, halos, width)

    m = mask[...][None]
    sums = [convolve(field_l, half, taps_f.at[0], pair, width) for half in range(2)]
    spreads = [convolve(field_e, half, taps_g.at[0], pair, width) for half in range(2)]
    errors = []
    for part in range(2):
        preact = to_native(sums[0], sums[1], part, width)
        spread = to_native(spreads[0], spreads[1], part, width)
        s = jax.nn.sigmoid(preact)
        inside = m * s
        silu = preact * inside
        shaped = silu.astype(BF).astype(F32)
        slope = inside + silu * (1.0 - s)
        restored[:, part] = (output_one[:, part].astype(F32) - shaped).astype(BF)
        total = (cotangent_one[:, part].astype(F32) + m * spread).astype(BF)
        grad[:, part] = total
        errors.append(total.astype(F32) * slope)
    write_parts(0, pair, errors, parts, depth)

    @pl.when(pair == depth // 2 - 1)
    def _():
        kept.wait()


def third_kernel(depth, width, mask, taps, centre, *refs):
    halos, cotangent_two, grad, field = refs[:4], refs[4], refs[5], refs[6]
    pair = pl.program_id(0)

    @pl.when(pair == 0)
    def _():
        build_field(field, 0, centre, halos, width)

    m = mask[...][None]
    sums = [convolve(field, half, taps.at[0], pair, width) for half in range(2)]
    for part in range(2):
        spread = to_native(sums[0], sums[1], part, width)
        grad[:, part] = (cotangent_two[:, part].astype(F32) + m * spread).astype(BF)


def conv_call(kernel, mask, matrices, centre, halos, natives, n_native_out, out_fields, fields, name):
    channels, depth, tall, width = natives[0].shape
    rows = channels * HALF
    length = matrices[0][0].shape[3]
    shapes = part_shapes(out_fields, channels, depth, width) if out_fields else []
    tap_specs = [
        fixed_spec((1, 3, rows, length), (k, 0, 0, 0)) for _, k in matrices
    ]
    native = natives[0].shape
    held = (2, length, (depth + 2) * width)
    export = 1 if out_fields else 0
    return pl.pallas_call(
        functools.partial(kernel, depth, width),
        out_shape=[jax.ShapeDtypeStruct(native, BF)] * n_native_out + [jax.ShapeDtypeStruct(s, BF) for s in shapes]
        + [jax.ShapeDtypeStruct(held, BF)] * export,
        grid=(depth // 2,),
        in_specs=[fixed_spec(mask.shape)]
        + tap_specs
        + [fixed_spec(centre.shape)]
        + [fixed_spec(h.shape) for h in halos]
        + [pair_spec(native)] * len(natives),
        out_specs=[pair_spec(native)] * n_native_out
        + (part_specs(shapes, width) if shapes else [])
        + [pl.BlockSpec(memory_space=pl.ANY)] * export,
        scratch_shapes=[pltpu.VMEM(held, BF)] * fields + [pltpu.SemaphoreType.DMA] * export,
        compiler_params=params(22 + 12 * (fields - 1)),
        cost_estimate=cost(2 * 2 * rows * 3 * length * depth * width * fields, 2e7),
        name=name,
    )(mask, *[streamed(m) for m, _ in matrices], centre, *halos, *[streamed(v) for v in natives])


def gradient_half_kernel(depth, width, field, errors, out):
    lanes = pl.ds(pl.multiple_of(pl.program_id(0) * width, width), depth * width)
    out[0] = lax.dot_general(
        errors[0, 0], field[0, :, lanes], (((1,), (1,)), ((), ())), preferred_element_type=F32
    )


def gradient_kernel(depth, width, field, errors, before, out, products):
    rows = errors.shape[2]
    channels = rows // HALF
    a = pl.program_id(0)
    lanes = pl.ds(pl.multiple_of(a * width, width), depth * width)

    products[...] = before[0] + lax.dot_general(
        errors[0, 0], field[0, :, lanes], (((1,), (1,)), ((), ())), preferred_element_type=F32
    )

    def pieces(value):
        high = value.astype(BF)
        return high, (value - high.astype(F32)).astype(BF)

    def tile(size):
        row = lax.broadcasted_iota(jnp.int32, (2 * HALF, size), 0) % HALF
        return row, lax.broadcasted_iota(jnp.int32, (2 * HALF, size), 1)

    gather_row = lax.broadcasted_iota(jnp.int32, (channels, rows), 0)
    gather_col = lax.broadcasted_iota(jnp.int32, (channels, rows), 1)
    gather = jnp.where(gather_col // HALF == gather_row, 1.0, 0.0).astype(BF)

    def chosen(parts, keep):
        total = None
        for part in parts:
            size = part.shape[1]
            kept = (part.reshape(rows // (2 * HALF), 2 * HALF, size) * keep[None]).reshape(rows, size)
            term = jnp.dot(gather, kept, preferred_element_type=F32)
            total = term if total is None else total + term
        return total

    row, col = tile(rows)
    bands = [jnp.where(col % HALF - row == b - 1, 1.0, 0.0).astype(BF) for b in range(3)]
    picked = {}
    for c in range(3):
        parts = pieces(products[:, c * rows : (c + 1) * rows])
        for b in range(3):
            picked[b, c] = chosen(parts, bands[b])
    row, col = tile(6 * channels)
    ends = jnp.where(row == jnp.where(col // channels % 2 == 0, 0, HALF - 1), 1.0, 0.0).astype(BF)
    sides = chosen(pieces(products[:, 3 * rows :]), ends)
    fold_row = lax.broadcasted_iota(jnp.int32, (rows, channels), 0)
    fold_col = lax.broadcasted_iota(jnp.int32, (rows, channels), 1)
    fold = jnp.where(fold_row // HALF == fold_col, 1.0, 0.0).astype(BF)
    summed = None
    for piece in pieces(jnp.concatenate([picked[b, c] for b in range(3) for c in range(3)], axis=0)):
        term = jnp.dot(piece, fold, preferred_element_type=F32)
        summed = term if summed is None else summed + term
    values = []
    for b in range(3):
        for c in range(3):
            at = (3 * b + c) * channels
            value = summed[at : at + channels]
            if b != 1:
                at = (2 * c + b // 2) * channels
                value = value + sides[:, at : at + channels]
            values.append(value)
    out[:, pl.ds(pl.multiple_of(a * 8 * channels, 8 * channels), 8 * channels)] = jnp.concatenate(values[:8], axis=1)
    empty = jnp.zeros((channels, channels), F32)
    tail = jnp.concatenate([jnp.where(a == k, values[8], empty) for k in range(3)] + [empty] * 5, axis=1)
    last = slice(24 * channels, 32 * channels)

    @pl.when(a == 0)
    def _():
        out[:, last] = tail

    @pl.when(a > 0)
    def _():
        out[:, last] = out[:, last] + tail


def weight_gradient(field, errors, which, half, width, before=None):
    _, length, columns = field.shape
    rows = errors.shape[2]
    channels = rows // HALF
    depth = errors.shape[3] // width
    raw = (3, rows, length)
    raw_spec = pl.BlockSpec((1, rows, length), lambda i: (i, 0, 0))
    last = before is not None
    result = (channels, 32 * channels) if last else raw
    return pl.pallas_call(
        functools.partial(gradient_kernel if last else gradient_half_kernel, depth, width),
        out_shape=jax.ShapeDtypeStruct(result, F32),
        grid=(3,),
        in_specs=[
            fixed_spec((1, length, columns), (half, 0, 0)),
            fixed_spec((1, 1, rows, depth * width), (which, half, 0, 0)),
        ]
        + [raw_spec] * last,
        out_specs=whole_spec(result) if last else raw_spec,
        scratch_shapes=[pltpu.VMEM((rows, length), F32)] * last,
        compiler_params=params(16),
        cost_estimate=cost(2 * rows * 3 * length * depth * width, 1e7),
        name="weight_gradient",
    )(*([field, errors] + [before] * last))


def unpack_kernel(packed, *outs):
    channels = packed.shape[0]
    fit = 128 // channels
    for k, out in enumerate(outs):
        for a in range(3):
            for t in range(9):
                at = 8 * a + t if t < 8 else 24 + a
                at += 32 * k
                lane = at % fit * channels
                out[9 * a + t] = packed[:, at // fit, lane : lane + channels]


def unpack(packed):
    channels = packed.shape[0]
    shape = (27, channels, channels)
    return pl.pallas_call(
        unpack_kernel,
        out_shape=[jax.ShapeDtypeStruct(shape, F32)] * 2,
        grid=(1,),
        in_specs=[whole_spec(packed.shape)],
        out_specs=[whole_spec(shape)] * 2,
        compiler_params=params(16),
        name="unpack",
    )(packed)


def total_over_devices(value, scale):
    axes = ("depth", "group")
    devices = lax.axis_size("depth") * lax.axis_size("group")
    shares = lax.all_to_all(value.reshape(devices, -1, 128), axes, 0, 0)
    share = jnp.sum(shares, axis=0) * scale
    everyone = lax.all_to_all(jnp.broadcast_to(share[None], shares.shape), axes, 0, 0)
    return everyone


def shift_along(value, axis, step):
    size = lax.axis_size(axis)
    return lax.ppermute(value, axis, [(i + step, i) for i in range(size) if 0 <= i + step < size])


def exchange_sides(faces):
    zlo, zhi, ylo, yhi = faces
    return shift_along(yhi, "group", -1), shift_along(ylo, "group", 1)


def exchange_faces(faces, sides, width):
    zlo, zhi, _, _ = faces
    low, high = sides
    first = jnp.concatenate([zlo, low[:, :, :width], high[:, :, :width]], axis=1)
    last = jnp.concatenate([zhi, low[:, :, -width:], high[:, :, -width:]], axis=1)
    return [shift_along(last, "depth", -1), shift_along(first, "depth", 1), low, high]


def after(value, others):
    return lax.optimization_barrier((value, others))[0]


def local(
    output_one, output_two, cotangent_one, cotangent_two, first_weight, second_weight, bricks
):
    brick_edge = output_one.shape[1]
    width = output_one.shape[3]
    slots = bricks.shape[2]
    groups = lax.axis_size("group")
    position = lax.axis_index("group")
    own_list = bricks[0][position]
    present = jnp.any(own_list[:, None] == jnp.arange(slots, dtype=jnp.int32)[None, :], axis=0)
    mask = jnp.repeat(present.astype(F32), brick_edge)[None, :]

    upper, *faces = upper_parts(output_one, mask)
    sides = exchange_sides(faces)

    def turned(kernel):
        return jnp.transpose(jnp.flip(kernel, 0), (0, 2, 1))

    taps_g = banded(jnp.stack([second_weight, turned(second_weight)]))
    sides = after(sides, taps_g)
    upper_halos = exchange_faces(faces, sides, width)
    taps_f = banded(jnp.stack([first_weight, turned(first_weight)]))

    restored_two, middle, *faces, field = conv_call(
        first_kernel, mask, [(taps_g, 0)], upper, upper_halos, [output_two, cotangent_two], 1, 2, 1, "first_conv"
    )
    sides = exchange_sides(faces)
    second_a = weight_gradient(field, middle, 1, 0, width)
    sides = after(sides, (second_a, taps_f))
    middle_halos = exchange_faces(faces, sides, width)
    second_total = weight_gradient(field, middle, 1, 1, width, second_a)
    restored_one, input_grad_one, last, *faces, field = conv_call(
        second_kernel,
        mask,
        [(taps_f, 0), (taps_g, 1)],
        middle,
        middle_halos,
        [output_one, cotangent_one],
        2,
        1,
        2,
        "second_conv",
    )
    sides = exchange_sides(faces)
    first_a = weight_gradient(field, last, 0, 0, width)
    sides = after(sides, first_a)
    last_halos = exchange_faces(faces, sides, width)
    first_total = weight_gradient(field, last, 0, 1, width, first_a)
    (input_grad_two,) = conv_call(
        third_kernel, mask, [(taps_f, 1)], last, last_halos, [cotangent_two], 1, 0, 1, "third_conv"
    )
    scale = 1.0 / math.sqrt(
        float(brick_edge * lax.axis_size("depth") * output_one.shape[2] * groups * width)
    )
    packed = jnp.concatenate([first_total, second_total], axis=1)
    first_total, second_total = unpack(total_over_devices(packed, scale).reshape(packed.shape[0], -1, 128))
    return (restored_one, restored_two, input_grad_one, input_grad_two, first_total, second_total)


def solution(mesh):
    slab = P(None, "depth", "group", None)
    return jax.shard_map(
        local,
        mesh=mesh,
        in_specs=(slab, slab, slab, slab, P(), P(), P("depth", None, None)),
        out_specs=(slab, slab, slab, slab, P(), P()),
        check_vma=False,
    )
```
